32 devices in a mesh: tile: 8 (over z, y), row: 4 (over x, core).
Axes of the slice: x: 2, y: 2, z: 4, core: 2. Of those that a mesh axis runs over, the one named last changes fastest.
Arguments:
- intensity: bfloat16 [8, 128, 11264], P('tile', 'row'), may hold values from 0.099609375 to 1
- volume: float32 [64, 128, 256], P('tile', 'row'), may hold values from 0 to 1
- footprint: bfloat16 [8, 256, 256], P('tile'), may hold values from 0.0010681152 to 0.021484375
- foot_offset: int32 [64, 8], replicated, may hold values from 2 to 84, as said below
- tile_count: int32 [8], replicated, may hold values from 1 to 8, as said below
Outputs:
- residual: float32 [8, 128, 11264], P('tile', 'row')
- correction: float32 [64, 128, 256], P('tile', 'row')
The draws below stay inside these ranges and needn't reach their ends.
Inputs may be any that keep to these rules, and one draw needn't show every extreme that they name: `foot_offset`: slot j belongs to group j // 8. At every angle the offsets of one group's slots differ by at most 3; wherever a group has two or more slots, by exactly 3. `tile_count`: some group has all its slots live.
All inputs are finite; a program needn't handle non-finite values.
Results may differ from the reference program's by a relative error of at most 0.00065.
Values may be sent and summed in bfloat16 or wider, within the bound.
No kernel may reach another device: no remote copies, remote signals or barrier semaphores. Data moves between devices by JAX's collectives and lax.ppermute only.
A program may use at most 128 MiB of HBM per device.

```python
import math
import jax
import jax.numpy as jnp
import numpy as np
from jax import lax

NCB = 88
CB = 128
TV = 256
SPREAD = 4
RIM = 3
SLOTS_DEV = 8
ANGLES = 8
ROWS = 128
TILE_SLOTS = 64
GROUPS = 8


def draw_foot_offset(key, part):
    base_key = jax.random.fold_in(key, 11)
    first_key, second_key, third_key = jax.random.split(base_key, 3)
    starts = jax.random.randint(first_key, (GROUPS, 1, ANGLES), 2, NCB - SPREAD - 2, dtype=jnp.int32)
    deltas = jax.random.randint(second_key, (GROUPS, SLOTS_DEV, ANGLES), 0, SPREAD, dtype=jnp.int32)
    slot_ids = jnp.arange(SLOTS_DEV, dtype=jnp.int32)[None, :, None]
    scores = jax.random.randint(third_key, (GROUPS, SLOTS_DEV, ANGLES), 0, 1 << 20, dtype=jnp.int32) * SLOTS_DEV + slot_ids
    ranked = jnp.argsort(scores, axis=1, stable=True).astype(jnp.int32)
    lowest = ranked[:, 0:1, :]
    highest = ranked[:, min(1, SLOTS_DEV - 1):min(2, SLOTS_DEV), :]
    deltas = jnp.where(slot_ids == highest, SPREAD - 1, deltas)
    deltas = jnp.where(slot_ids == lowest, 0, deltas)
    return (starts + deltas).reshape(TILE_SLOTS, ANGLES)


def draw_tile_count(key, part):
    base_key = jax.random.fold_in(key, 23)
    first_key, second_key = jax.random.split(base_key)
    counts = jax.random.randint(first_key, (GROUPS,), 1, SLOTS_DEV + 1, dtype=jnp.int32)
    fullest = jax.random.randint(second_key, (), 0, GROUPS, dtype=jnp.int32)
    return jnp.where(jnp.arange(GROUPS, dtype=jnp.int32) == fullest, SLOTS_DEV, counts)


def shard_levels(own_key, extent, shards, least, largest):
    factor_of = 1.0
    for dim, parts in shards:
        steps = jax.random.uniform(jax.random.fold_in(jax.random.fold_in(own_key, 6), dim), (parts,), jnp.float32, least / len(shards), largest / len(shards))
        factor_of = factor_of * jnp.repeat(jnp.exp(steps), extent[dim] // parts).reshape((-1,) + (1,) * (len(extent) - 1 - dim))
    return factor_of


def setup_inputs(seed: int = 0) -> dict:
    keys = jax.random.split(jax.random.key(seed), 6)
    return {
        "intensity": jnp.clip(jnp.exp(math.log(1.0) - 2.306499 * jax.random.uniform(keys[0], (ANGLES, ROWS, NCB * CB), jnp.float32) ** shard_levels(keys[0], (ANGLES, ROWS, NCB * CB), ((0, 8), (1, 4)), -0.2, 0.2)), 0.099609375, 1.0).astype(jnp.bfloat16),
        "volume": jnp.clip(1.0 * jax.random.uniform(keys[1], (TILE_SLOTS, ROWS, TV), jnp.float32) ** shard_levels(keys[1], (TILE_SLOTS, ROWS, TV), ((0, 8), (1, 4)), -0.2, 0.2), 0.0, 1.0),
        "footprint": jnp.clip(jnp.exp(math.log(0.021484375) - 3.0014303 * jax.random.uniform(keys[2], (ANGLES, TV, 2 * CB), jnp.float32) ** shard_levels(keys[2], (ANGLES, TV, 2 * CB), ((0, 8),), -0.2, 0.2)), 0.0010681152, 0.021484375).astype(jnp.bfloat16),
        "foot_offset": draw_foot_offset(jax.random.fold_in(keys[5], 71), 0),
        "tile_count": draw_tile_count(jax.random.fold_in(keys[5], 71), 0),
    }


decay_length = 2.0
row_floor = 0.5


def smoothing_taps():
    spread_taps = np.exp(-np.abs(np.arange(-RIM, RIM + 1)) / decay_length)
    return spread_taps / spread_taps.sum()


def retrieve_phase(intensity):
    tap_weights = smoothing_taps()
    height_rows = intensity.shape[1]
    column_count = intensity.shape[2]
    padded = jnp.pad(intensity.astype(jnp.float32), ((0, 0), (RIM, RIM), (0, 0)))
    across = float(tap_weights[0]) * padded[:, 0:height_rows, :]
    for tap_index in range(1, 2 * RIM + 1):
        across = across + float(tap_weights[tap_index]) * padded[:, tap_index:tap_index + height_rows, :]
    widened = jnp.pad(across, ((0, 0), (0, 0), (RIM, RIM)))
    smoothed = float(tap_weights[0]) * widened[:, :, 0:column_count]
    for tap_index in range(1, 2 * RIM + 1):
        smoothed = smoothed + float(tap_weights[tap_index]) * widened[:, :, tap_index:tap_index + column_count]
    return -jnp.log(smoothed)


def reference(intensity, volume, footprint, foot_offset, tile_count):
    phase_map = retrieve_phase(intensity)
    slot_ids = jnp.arange(TILE_SLOTS, dtype=jnp.int32)
    repeated = jnp.broadcast_to(tile_count[:, None], (GROUPS, SLOTS_DEV)).reshape(TILE_SLOTS)
    live = (slot_ids % SLOTS_DEV < repeated).astype(jnp.float32)
    masked = volume * live[:, None, None]
    table_all = footprint.astype(jnp.float32)
    column_sums = jnp.sum(table_all, axis=(0, 2))
    block_ids = jnp.arange(NCB, dtype=jnp.int32)

    def one_angle(running, inputs):
        table_one, offsets, phase_one = inputs
        load_blocks = jax.ops.segment_sum(masked, offsets, num_segments=NCB)
        load_half = lax.optimization_barrier(load_blocks.astype(jnp.bfloat16)).astype(jnp.float32)
        images = jnp.einsum('brv,vc->rbc', load_half, table_one)
        leading = images[:, :, :CB]
        trailing = jnp.concatenate([jnp.zeros_like(images[:, :1, CB:]), images[:, :-1, CB:]], axis=1)
        projection = (leading + trailing).reshape(ROWS, NCB * CB)
        voxel_sums = jnp.sum(table_one, axis=0)
        counts = jnp.sum((offsets[:, None] == block_ids[None, :]).astype(jnp.float32) * live[:, None], axis=0)
        row_first = counts[:, None] * voxel_sums[None, :CB]
        row_second = counts[:, None] * voxel_sums[None, CB:]
        row_second = jnp.concatenate([jnp.zeros_like(row_second[:1]), row_second[:-1]], axis=0)
        row_sums = (row_first + row_second).reshape(NCB * CB)
        residual = phase_one - projection
        weighted = lax.optimization_barrier((residual / jnp.maximum(row_sums, row_floor)).astype(jnp.bfloat16)).astype(jnp.float32)
        halves = weighted.reshape(ROWS, NCB, CB)
        nearer = jnp.einsum('rbc,vc->brv', halves, table_one[:, :CB])
        farther = jnp.einsum('rbc,vc->brv', halves, table_one[:, CB:])
        farther = jnp.concatenate([farther[1:], jnp.zeros_like(farther[:1])], axis=0)
        back_blocks = nearer + farther
        running = running + jnp.take(back_blocks, offsets, axis=0)
        return running, residual

    start_sum = jnp.zeros((TILE_SLOTS, ROWS, TV), jnp.float32)
    summed, residual = lax.scan(one_angle, start_sum, (table_all, jnp.transpose(foot_offset), phase_map))
    correction = summed * live[:, None, None] / column_sums[None, None, :]
    return residual, correction
```

```python
import jax
import jax.numpy as jnp
import numpy as np
from jax import lax
from jax.experimental import pallas as pl
from jax.experimental.pallas import tpu as pltpu
from jax.sharding import PartitionSpec as P


SPREAD = 4
RIM = 3
DIRECT_LIMIT = 16
EXTRA_ROWS = 8
SUM_SCALE = 2048.0
LOW_SCALE = 32000.0
CODE_TOP = 32000.0

decay_length = 2.0
row_floor = 0.5


SMEM = pl.BlockSpec(memory_space=pltpu.SMEM)
VMEM = pl.BlockSpec(memory_space=pltpu.VMEM)


def params(mib):
    return pltpu.CompilerParams(vmem_limit_bytes=mib << 20)


def halo_rows(block, width):
    count = lax.axis_size("row")
    forward = [(i, i + 1) for i in range(count - 1)]
    backward = [(target, source) for source, target in forward]
    rows = block.shape[1]
    low = lax.ppermute(block[:, rows - width :], "row", forward)
    high = lax.ppermute(block[:, :width], "row", backward)
    return low, high


def smoothing_taps():
    spread_taps = np.exp(-np.abs(np.arange(-RIM, RIM + 1)) / decay_length)
    return spread_taps / spread_taps.sum()


def retrieve_phase(intensity):
    low, high = halo_rows(intensity, RIM)
    padded = jnp.concatenate([low, intensity, high], axis=1)
    tap_weights = smoothing_taps()
    height_rows = intensity.shape[1]
    column_count = intensity.shape[2]
    across = float(tap_weights[0]) * padded[:, 0:height_rows, :].astype(jnp.float32)
    for tap_index in range(1, 2 * RIM + 1):
        across = across + float(tap_weights[tap_index]) * padded[
            :, tap_index : tap_index + height_rows, :
        ].astype(jnp.float32)
    widened = jnp.pad(across, ((0, 0), (0, 0), (RIM, RIM)))
    smoothed = float(tap_weights[0]) * widened[:, :, 0:column_count]
    for tap_index in range(1, 2 * RIM + 1):
        smoothed = (
            smoothed
            + float(tap_weights[tap_index]) * widened[:, :, tap_index : tap_index + column_count]
        )
    return -jnp.log(smoothed)


def each_piece(direct, count, member, refs, body):
    if direct:
        for k in range(count):
            body(refs[k], member ^ k)
    else:

        def step(k, carry):
            body(refs[0].at[k], k)
            return carry

        lax.fori_loop(0, count, step, 0)


def group_start(offsets, angle, group, slots):
    low = offsets[angle, group * slots]
    for j in range(1, slots):
        low = jnp.minimum(low, offsets[angle, group * slots + j])
    return low


def load_kernel(direct, count, slots, offsets, tile_count, volume, *pieces):
    member = lax.axis_index("tile")
    live = tile_count[member]

    def one(piece, angle):
        start = group_start(offsets, angle, member, slots)
        places = [offsets[angle, member * slots + j] - start for j in range(slots)]
        places = [jnp.where(j < live, places[j], -1) for j in range(slots)]
        for s in range(SPREAD):
            total = jnp.zeros(volume.shape[1:], jnp.float32)
            for j in range(slots):
                total = total + jnp.where(places[j] == s, 1.0, 0.0) * volume[j]
            piece[s] = total.astype(piece.dtype)

    each_piece(direct, count, member, pieces, one)


def table_kernel(slots, blocks, offsets, tile_count, offset_rows, footprint, inverse, sums):
    member = lax.axis_index("tile")
    half = footprint.shape[1] // 2
    padded = inverse.shape[0]
    total = offset_rows.shape[1]
    table = footprint[...]
    by_column = jnp.sum(table.astype(jnp.float32), axis=0, keepdims=True)
    mine = offset_rows[pl.ds(member, 1), :]
    lane = lax.broadcasted_iota(jnp.int32, (1, total), 1)
    alive = jnp.zeros((1, total), jnp.float32)
    for g in range(total // slots):
        here = (lane >= g * slots) & (lane < g * slots + tile_count[g])
        alive = jnp.where(here, 1.0, alive)
    block = lax.broadcasted_iota(jnp.int32, (padded, total), 0)
    hits = jnp.where(block == mine, alive, 0.0)
    counts = jnp.sum(hits, axis=1, keepdims=True)
    before = jnp.sum(jnp.where(block == mine + 1, alive, 0.0), axis=1, keepdims=True)
    rows = counts * by_column[:, :half] + before * by_column[:, half:]
    inside = lax.broadcasted_iota(jnp.int32, (padded, half), 0) < blocks
    inverse[...] = jnp.where(inside, 1.0 / jnp.maximum(rows, row_floor), 0.0)
    ones = jnp.ones((8, table.shape[1]), table.dtype)
    by_voxel = lax.dot_general(
        ones, table, (((1,), (1,)), ((), ())), preferred_element_type=jnp.float32
    )[0:1]
    scaled = by_voxel * SUM_SCALE
    whole = jnp.floor(scaled)
    low = jnp.floor((scaled - whole) * LOW_SCALE + 0.5)
    packed = jnp.concatenate(
        [whole[:, :half], whole[:, half:], low[:, :half], low[:, half:]], axis=0
    )
    sums[...] = jnp.concatenate([packed, jnp.zeros((4, half), jnp.float32)], axis=0)


def angle_kernel(direct, count, slots, offsets, phase, footprint, inverse, sums, *refs):
    lists = count if direct else 1
    arrived, residual, sent, windows = (
        refs[:lists],
        refs[lists],
        refs[lists + 1 : 2 * lists + 1],
        refs[2 * lists + 1],
    )
    member = lax.axis_index("tile")
    table = footprint[...]
    rows, columns = phase.shape
    voxels = footprint.shape[0]
    half = footprint.shape[1] // 2
    blocks = columns // half
    residual[...] = phase[...]

    def subtract(piece, group):
        start = group_start(offsets, member, group, slots)
        image = jnp.dot(
            piece[...].reshape(SPREAD * rows, voxels), table, preferred_element_type=jnp.float32
        )
        for s in range(SPREAD + 1):
            part = None
            if s < SPREAD:
                part = image[s * rows : (s + 1) * rows, :half]
            if s > 0:
                far = image[(s - 1) * rows : s * rows, half:]
                part = far if part is None else part + far
            block = jnp.minimum(start + s, blocks - 1)
            if s >= SPREAD - 1:
                part = jnp.where(start + s < blocks, part, 0.0)
            at = pl.ds(pl.multiple_of(block * half, half), half)
            residual[:, at] = residual[:, at] - part

    each_piece(direct, count, member, arrived, subtract)

    def send(piece, group):
        start = group_start(offsets, member, group, slots)
        for s in range(SPREAD + 1):
            block = jnp.minimum(start + s, blocks - 1)
            at = pl.ds(pl.multiple_of(block * half, half), half)
            scale = inverse[pl.ds(start + s, 1), :]
            windows[:, s * half : (s + 1) * half] = (residual[:, at] * scale).astype(windows.dtype)
        stacked = jnp.concatenate(
            [windows[:, s * half : (s + 2) * half] for s in range(SPREAD)], axis=0
        )
        back = lax.dot_general(
            stacked, table, (((1,), (1,)), ((), ())), preferred_element_type=jnp.float32
        )
        top = jnp.max(jnp.max(jnp.abs(back), axis=1, keepdims=True), axis=0, keepdims=True)
        power = jnp.floor(jnp.log2(CODE_TOP / jnp.maximum(top, 1e-30)))
        code = jnp.round(back * jnp.exp2(power)).astype(jnp.int32)
        for s in range(SPREAD):
            for h in range(2):
                base = (2 * s + h) * rows
                piece[base : base + rows, :] = code[
                    s * rows : (s + 1) * rows, h * half : (h + 1) * half
                ].astype(piece.dtype)
        base = 2 * SPREAD * rows
        line = lax.broadcasted_iota(jnp.int32, (EXTRA_ROWS, half), 0)
        extra = jnp.where(line < 4, sums[...], jnp.broadcast_to(power, (EXTRA_ROWS, half)))
        piece[base : base + EXTRA_ROWS, :] = extra.astype(jnp.int32).astype(piece.dtype)

    each_piece(direct, count, member, sent, send)


def gather_kernel(direct, count, slots, rows, offsets, tile_count, *refs):
    lists = count if direct else 1
    received, correction, decoded, column_sums = (
        refs[:lists],
        refs[lists],
        refs[lists + 1],
        refs[lists + 2],
    )
    member = lax.axis_index("tile")
    live = tile_count[member]
    half = column_sums.shape[1]
    base = 2 * SPREAD * rows
    column_sums[...] = jnp.zeros_like(column_sums)
    correction[...] = jnp.zeros_like(correction)

    def one(piece, angle):
        extra = piece[base : base + EXTRA_ROWS, :].astype(jnp.float32)
        column_sums[...] += (extra[0:2] + extra[2:4] * (1.0 / LOW_SCALE)) * (1.0 / SUM_SCALE)
        scale = jnp.exp2(-extra[4:5])
        start = group_start(offsets, angle, member, slots)
        decoded[...] = piece[0:base, :].astype(jnp.float32) * scale
        for j in range(slots):
            place = offsets[angle, member * slots + j] - start
            at = pl.multiple_of(place * (2 * rows), 2 * rows)
            for h in range(2):
                correction[j, :, h * half : (h + 1) * half] += decoded[
                    pl.ds(at + h * rows, rows), :
                ]

    each_piece(direct, count, member, received, one)
    inverse = 1.0 / column_sums[...]
    for j in range(slots):
        weight = jnp.where(j < live, 1.0, 0.0)
        for h in range(2):
            part = correction[j, :, h * half : (h + 1) * half]
            correction[j, :, h * half : (h + 1) * half] = part * (inverse[h : h + 1] * weight)


def exchange(direct, count, pieces):
    if not direct:
        return [lax.all_to_all(pieces[0], "tile", split_axis=0, concat_axis=0, tiled=True)]
    arrived = [pieces[0]]
    for k in range(1, count):
        arrived.append(lax.ppermute(pieces[k], "tile", [(i, i ^ k) for i in range(count)]))
    return arrived


def use_direct(count):
    return count <= DIRECT_LIMIT and count & (count - 1) == 0


def local(intensity, volume, footprint, foot_offset, tile_count):
    count = lax.axis_size("tile")
    direct = use_direct(count)
    slots, rows, voxels = volume.shape
    angles_here, _, window = footprint.shape
    assert angles_here == 1
    half = window // 2
    columns = intensity.shape[2]
    blocks = columns // half
    padded_blocks = -(-(blocks + SPREAD + 1) // 8) * 8
    offsets = jnp.transpose(foot_offset)
    table = footprint[0]

    def piece_shapes(shape, dtype):
        if direct:
            return [jax.ShapeDtypeStruct(shape, dtype)] * count
        return [jax.ShapeDtypeStruct((count,) + shape, dtype)]

    load_shapes = piece_shapes((SPREAD, rows, voxels), jnp.bfloat16)
    loads = pl.pallas_call(
        lambda *refs: load_kernel(direct, count, slots, *refs),
        out_shape=load_shapes,
        in_specs=[SMEM, SMEM, VMEM],
        out_specs=[VMEM] * len(load_shapes),
        compiler_params=params(16),
        name="loads",
    )(offsets, tile_count, volume)
    arrived = exchange(direct, count, loads)

    phase_map = retrieve_phase(intensity)[0]
    inverse, sums = pl.pallas_call(
        lambda *refs: table_kernel(slots, blocks, *refs),
        out_shape=[
            jax.ShapeDtypeStruct((padded_blocks, half), jnp.float32),
            jax.ShapeDtypeStruct((EXTRA_ROWS, half), jnp.float32),
        ],
        in_specs=[SMEM, SMEM, VMEM, VMEM],
        out_specs=[VMEM, VMEM],
        compiler_params=params(16),
        name="tables",
    )(offsets, tile_count, offsets, table)

    back_shapes = piece_shapes((2 * SPREAD * rows + EXTRA_ROWS, half), jnp.int16)
    residual, *backs = pl.pallas_call(
        lambda *refs: angle_kernel(direct, count, slots, *refs),
        out_shape=[jax.ShapeDtypeStruct((rows, columns), jnp.float32)] + back_shapes,
        in_specs=[SMEM] + [VMEM] * (4 + len(arrived)),
        out_specs=[VMEM] * (1 + len(back_shapes)),
        scratch_shapes=[pltpu.VMEM((rows, (SPREAD + 1) * half), jnp.bfloat16)],
        compiler_params=params(24),
        name="angle",
    )(offsets, phase_map, table, inverse, sums, *arrived)
    received = exchange(direct, count, backs)

    correction = pl.pallas_call(
        lambda *refs: gather_kernel(direct, count, slots, rows, *refs),
        out_shape=jax.ShapeDtypeStruct((slots, rows, voxels), jnp.float32),
        in_specs=[SMEM, SMEM] + [VMEM] * len(received),
        out_specs=VMEM,
        scratch_shapes=[
            pltpu.VMEM((2 * SPREAD * rows, half), jnp.float32),
            pltpu.VMEM((2, half), jnp.float32),
        ],
        compiler_params=params(16),
        name="gather",
    )(offsets, tile_count, *received)
    return residual[None], correction


def solution(mesh):
    placed = (P("tile", "row", None), P("tile", "row", None), P("tile", None, None), P(), P())
    return jax.shard_map(
        local,
        mesh=mesh,
        in_specs=placed,
        out_specs=(P("tile", "row", None), P("tile", "row", None)),
        check_vma=False,
    )
```

```python
import jax
import jax.numpy as jnp
import numpy as np
from jax import lax
from jax.experimental import pallas as pl
from jax.experimental.pallas import tpu as pltpu
from jax.sharding import PartitionSpec as P


SPREAD = 4
RIM = 3
HALO = 8
TALL = 256
WIDE = 1024
DIRECT_LIMIT = 16
EXTRA_ROWS = 8
SUM_SCALE = 2048.0
LOW_SCALE = 32000.0
CODE_TOP = 32000.0

decay_length = 2.0
row_floor = 0.5


SMEM = pl.BlockSpec(memory_space=pltpu.SMEM)
VMEM = pl.BlockSpec(memory_space=pltpu.VMEM)
HBM = pl.BlockSpec(memory_space=pltpu.HBM)


def params(mib):
    return pltpu.CompilerParams(vmem_limit_bytes=mib << 20)


def smoothing_taps():
    spread_taps = np.exp(-np.abs(np.arange(-RIM, RIM + 1)) / decay_length)
    return spread_taps / spread_taps.sum()


def each_piece(direct, count, member, refs, body):
    if direct:
        for k in range(count):
            body(refs[k], member ^ k)
    else:

        def step(k, carry):
            body(refs[0].at[k], k)
            return carry

        lax.fori_loop(0, count, step, 0)


def group_start(offsets, angle, group, slots):
    low = offsets[angle, group * slots]
    for j in range(1, slots):
        low = jnp.minimum(low, offsets[angle, group * slots + j])
    return low


def load_kernel(direct, count, slots, offsets_in, count_in, volume_in, table_in, intensity, *refs):
    lists = count if direct else 1
    near_rows, far_rows, table_out, offsets_out, count_out = refs[:5]
    pieces = refs[5 : 5 + lists]
    offsets, tile_count, volume, sems = refs[5 + lists :]
    member = lax.axis_index("tile")
    even = lax.rem(lax.axis_index("row"), 2) == 0
    last = intensity.shape[0] - HALO
    first_copy = pltpu.make_async_copy(offsets_in, offsets, sems.at[0])
    count_copy = pltpu.make_async_copy(count_in, tile_count, sems.at[1])
    volume_copy = pltpu.make_async_copy(volume_in, volume, sems.at[2])
    near = pl.multiple_of(jnp.where(even, last, 0), HALO)
    far = pl.multiple_of(jnp.where(even, 0, last), HALO)
    near_copy = pltpu.make_async_copy(intensity.at[pl.ds(near, HALO)], near_rows, sems.at[3])
    far_copy = pltpu.make_async_copy(intensity.at[pl.ds(far, HALO)], far_rows, sems.at[4])
    later = [near_copy, far_copy]
    for i, (here, there) in enumerate(
        ((table_in, table_out), (offsets_in, offsets_out), (count_in, count_out))
    ):
        later.append(pltpu.make_async_copy(here, there, sems.at[5 + i]))
    first_copy.start()
    count_copy.start()
    volume_copy.start()
    for copy in later:
        copy.start()
    first_copy.wait()
    count_copy.wait()
    live = tile_count[member]
    volume_copy.wait()

    def one(piece, angle):
        start = group_start(offsets, angle, member, slots)
        places = [offsets[angle, member * slots + j] - start for j in range(slots)]
        places = [jnp.where(j < live, places[j], -1) for j in range(slots)]
        for s in range(SPREAD):
            total = jnp.zeros(volume.shape[1:], jnp.float32)
            for j in range(slots):
                total = total + jnp.where(places[j] == s, 1.0, 0.0) * volume[j]
            piece[s] = total.astype(piece.dtype)

    each_piece(direct, count, member, pieces, one)
    for copy in later:
        copy.wait()


def tables(slots, blocks, offset_rows, tile_count, table, inverse, sums):
    member = lax.axis_index("tile")
    half = table.shape[1] // 2
    padded = inverse.shape[0]
    total = offset_rows.shape[1]
    by_column = jnp.sum(table.astype(jnp.float32), axis=0, keepdims=True)
    mine = offset_rows[pl.ds(member, 1), :]
    lane = lax.broadcasted_iota(jnp.int32, (1, total), 1)
    alive = jnp.zeros((1, total), jnp.float32)
    for g in range(total // slots):
        here = (lane >= g * slots) & (lane < g * slots + tile_count[g])
        alive = jnp.where(here, 1.0, alive)
    block = lax.broadcasted_iota(jnp.int32, (padded, total), 0)
    hits = jnp.where(block == mine, alive, 0.0)
    counts = jnp.sum(hits, axis=1, keepdims=True)
    before = jnp.sum(jnp.where(block == mine + 1, alive, 0.0), axis=1, keepdims=True)
    rows = counts * by_column[:, :half] + before * by_column[:, half:]
    inside = lax.broadcasted_iota(jnp.int32, (padded, half), 0) < blocks
    inverse[...] = jnp.where(inside, 1.0 / jnp.maximum(rows, row_floor), 0.0)
    ones = jnp.ones((8, table.shape[1]), table.dtype)
    by_voxel = lax.dot_general(
        ones, table, (((1,), (1,)), ((), ())), preferred_element_type=jnp.float32
    )[0:1]
    scaled = by_voxel * SUM_SCALE
    whole = jnp.floor(scaled)
    low = jnp.floor((scaled - whole) * LOW_SCALE + 0.5)
    packed = jnp.concatenate(
        [whole[:, :half], whole[:, half:], low[:, :half], low[:, half:]], axis=0
    )
    sums[...] = jnp.concatenate([packed, jnp.zeros((4, half), jnp.float32)], axis=0)


def spread_sum(x, axis, decay):
    size = x.shape[axis]
    down = x + decay * pltpu.roll(x, 1, axis)
    down = down + decay**2 * pltpu.roll(down, 2, axis)
    up = x + decay * pltpu.roll(x, size - 1, axis)
    up = up + decay**2 * pltpu.roll(up, size - 2, axis)
    return down + up - x


def phase_kernel(
    slots, tile_count, offset_rows, intensity, near_rows, far_rows, footprint, *refs
):
    phase, inverse, sums, across = refs
    rows, columns = intensity.shape
    half = footprint.shape[1] // 2
    blocks = columns // half
    tables(slots, blocks, offset_rows, tile_count, footprint[...], inverse, sums)
    even = lax.rem(lax.axis_index("row"), 2) == 0
    decay = float(np.exp(-1.0 / decay_length))
    centre = float(smoothing_taps()[RIM])
    across[:, :half] = jnp.zeros((rows, half), jnp.float32)
    across[:, half + columns :] = jnp.zeros((rows, half), jnp.float32)

    def vertical(step, carry):
        at = pl.ds(pl.multiple_of(step * TALL, half), TALL)
        near = near_rows[:, at].astype(jnp.float32)
        far = far_rows[:, at].astype(jnp.float32)
        x = jnp.concatenate(
            [
                jnp.where(even, far, near),
                intensity[:, at].astype(jnp.float32),
                jnp.where(even, near, far),
            ],
            axis=0,
        )
        filtered = spread_sum(x, 0, decay)[HALO : HALO + rows]
        across[:, pl.ds(pl.multiple_of(step * TALL + half, half), TALL)] = filtered
        return carry

    lax.fori_loop(0, columns // TALL, vertical, 0)

    def horizontal(step, carry):
        base = pl.multiple_of(step * WIDE, half)
        x = across[:, pl.ds(base, WIDE + 2 * half)]
        filtered = spread_sum(x, 1, decay)[:, half : half + WIDE]
        phase[:, pl.ds(base, WIDE)] = -jnp.log(filtered * centre**2)
        return carry

    lax.fori_loop(0, columns // WIDE, horizontal, 0)


def angle_kernel(direct, count, slots, offsets, phase, footprint, inverse, sums, *refs):
    lists = count if direct else 1
    arrived, residual, sent, windows = (
        refs[:lists],
        refs[lists],
        refs[lists + 1 : 2 * lists + 1],
        refs[2 * lists + 1],
    )
    member = lax.axis_index("tile")
    table = footprint[...]
    rows, columns = phase.shape
    voxels = footprint.shape[0]
    half = footprint.shape[1] // 2
    blocks = columns // half
    residual[...] = phase[...]

    def subtract(piece, group):
        start = group_start(offsets, member, group, slots)
        image = jnp.dot(
            piece[...].reshape(SPREAD * rows, voxels), table, preferred_element_type=jnp.float32
        )
        for s in range(SPREAD + 1):
            part = None
            if s < SPREAD:
                part = image[s * rows : (s + 1) * rows, :half]
            if s > 0:
                far = image[(s - 1) * rows : s * rows, half:]
                part = far if part is None else part + far
            block = jnp.minimum(start + s, blocks - 1)
            if s >= SPREAD - 1:
                part = jnp.where(start + s < blocks, part, 0.0)
            at = pl.ds(pl.multiple_of(block * half, half), half)
            residual[:, at] = residual[:, at] - part

    each_piece(direct, count, member, arrived, subtract)

    def send(piece, group):
        start = group_start(offsets, member, group, slots)
        for s in range(SPREAD + 1):
            block = jnp.minimum(start + s, blocks - 1)
            at = pl.ds(pl.multiple_of(block * half, half), half)
            scale = inverse[pl.ds(start + s, 1), :]
            windows[:, s * half : (s + 1) * half] = (residual[:, at] * scale).astype(windows.dtype)
        stacked = jnp.concatenate(
            [windows[:, s * half : (s + 2) * half] for s in range(SPREAD)], axis=0
        )
        back = lax.dot_general(
            stacked, table, (((1,), (1,)), ((), ())), preferred_element_type=jnp.float32
        )
        top = jnp.max(jnp.max(jnp.abs(back), axis=1, keepdims=True), axis=0, keepdims=True)
        power = jnp.floor(jnp.log2(CODE_TOP / jnp.maximum(top, 1e-30)))
        code = jnp.round(back * jnp.exp2(power)).astype(jnp.int32)
        for s in range(SPREAD):
            for h in range(2):
                base = (2 * s + h) * rows
                piece[base : base + rows, :] = code[
                    s * rows : (s + 1) * rows, h * half : (h + 1) * half
                ].astype(piece.dtype)
        base = 2 * SPREAD * rows
        line = lax.broadcasted_iota(jnp.int32, (EXTRA_ROWS, half), 0)
        extra = jnp.where(line < 4, sums[...], jnp.broadcast_to(power, (EXTRA_ROWS, half)))
        piece[base : base + EXTRA_ROWS, :] = extra.astype(jnp.int32).astype(piece.dtype)

    each_piece(direct, count, member, sent, send)


def gather_kernel(direct, count, slots, rows, offsets, tile_count, *refs):
    lists = count if direct else 1
    received, correction, decoded, column_sums = (
        refs[:lists],
        refs[lists],
        refs[lists + 1],
        refs[lists + 2],
    )
    member = lax.axis_index("tile")
    live = tile_count[member]
    half = column_sums.shape[1]
    base = 2 * SPREAD * rows
    column_sums[...] = jnp.zeros_like(column_sums)
    correction[...] = jnp.zeros_like(correction)

    def one(piece, angle):
        extra = piece[base : base + EXTRA_ROWS, :].astype(jnp.float32)
        column_sums[...] += (extra[0:2] + extra[2:4] * (1.0 / LOW_SCALE)) * (1.0 / SUM_SCALE)
        scale = jnp.exp2(-extra[4:5])
        start = group_start(offsets, angle, member, slots)
        decoded[...] = piece[0:base, :].astype(jnp.float32) * scale
        for j in range(slots):
            place = offsets[angle, member * slots + j] - start
            at = pl.multiple_of(place * (2 * rows), 2 * rows)
            for h in range(2):
                correction[j, :, h * half : (h + 1) * half] += decoded[
                    pl.ds(at + h * rows, rows), :
                ]

    each_piece(direct, count, member, received, one)
    inverse = 1.0 / column_sums[...]
    for j in range(slots):
        weight = jnp.where(j < live, 1.0, 0.0)
        for h in range(2):
            part = correction[j, :, h * half : (h + 1) * half]
            correction[j, :, h * half : (h + 1) * half] = part * (inverse[h : h + 1] * weight)


def exchange(direct, count, pieces):
    if not direct:
        return [lax.all_to_all(pieces[0], "tile", split_axis=0, concat_axis=0, tiled=True)]
    arrived = [pieces[0]]
    for k in range(1, count):
        arrived.append(lax.ppermute(pieces[k], "tile", [(i, i ^ k) for i in range(count)]))
    return arrived


def swap_halos(near_rows, far_rows):
    count = lax.axis_size("row")
    pairs = [(i, i + 1) for i in range(0, count - 1, 2)]
    between = [(i, i + 1) for i in range(1, count - 1, 2)]
    far_rows = lax.ppermute(far_rows, "row", between + [(b, a) for a, b in between])
    near_rows = lax.ppermute(near_rows, "row", pairs + [(b, a) for a, b in pairs])
    return near_rows, far_rows


def use_direct(count):
    return count <= DIRECT_LIMIT and count & (count - 1) == 0


def local(intensity, volume, footprint, foot_offset, tile_count):
    count = lax.axis_size("tile")
    direct = use_direct(count)
    slots, rows, voxels = volume.shape
    angles_here, _, window = footprint.shape
    assert angles_here == 1
    half = window // 2
    columns = intensity.shape[2]
    blocks = columns // half
    padded_blocks = -(-(blocks + SPREAD + 1) // 8) * 8
    offsets = jnp.transpose(foot_offset)
    table = footprint[0]

    def piece_shapes(shape, dtype):
        if direct:
            return [jax.ShapeDtypeStruct(shape, dtype)] * count
        return [jax.ShapeDtypeStruct((count,) + shape, dtype)]

    halo_shape = jax.ShapeDtypeStruct((HALO, columns), intensity.dtype)
    load_shapes = piece_shapes((SPREAD, rows, voxels), jnp.bfloat16)
    near_rows, far_rows, table, offsets_here, counts_here, *loads = pl.pallas_call(
        lambda *refs: load_kernel(direct, count, slots, *refs),
        out_shape=[halo_shape, halo_shape]
        + [jax.ShapeDtypeStruct(x.shape, x.dtype) for x in (table, offsets, tile_count)]
        + load_shapes,
        in_specs=[HBM] * 5,
        out_specs=[VMEM] * (5 + len(load_shapes)),
        scratch_shapes=[
            pltpu.SMEM(offsets.shape, jnp.int32),
            pltpu.SMEM(tile_count.shape, jnp.int32),
            pltpu.VMEM(volume.shape, volume.dtype),
            pltpu.SemaphoreType.DMA((8,)),
        ],
        compiler_params=params(16),
        name="loads",
    )(*[pltpu.with_memory_space_constraint(x, pltpu.HBM) for x in (offsets, tile_count, volume, table, intensity[0])])
    arrived = exchange(direct, count, loads)
    near_rows, far_rows = swap_halos(near_rows, far_rows)

    phase_map, inverse, sums = pl.pallas_call(
        lambda *refs: phase_kernel(slots, *refs),
        out_shape=[
            jax.ShapeDtypeStruct((rows, columns), jnp.float32),
            jax.ShapeDtypeStruct((padded_blocks, half), jnp.float32),
            jax.ShapeDtypeStruct((EXTRA_ROWS, half), jnp.float32),
        ],
        in_specs=[SMEM] + [VMEM] * 5,
        out_specs=[VMEM] * 3,
        scratch_shapes=[pltpu.VMEM((rows, columns + 2 * half), jnp.float32)],
        compiler_params=params(16),
        name="phase",
    )(counts_here, offsets_here, intensity[0], near_rows, far_rows, table)

    back_shapes = piece_shapes((2 * SPREAD * rows + EXTRA_ROWS, half), jnp.int16)
    residual, *backs = pl.pallas_call(
        lambda *refs: angle_kernel(direct, count, slots, *refs),
        out_shape=[jax.ShapeDtypeStruct((rows, columns), jnp.float32)] + back_shapes,
        in_specs=[SMEM] + [VMEM] * (4 + len(arrived)),
        out_specs=[VMEM] * (1 + len(back_shapes)),
        scratch_shapes=[pltpu.VMEM((rows, (SPREAD + 1) * half), jnp.bfloat16)],
        compiler_params=params(24),
        name="angle",
    )(offsets_here, phase_map, table, inverse, sums, *arrived)
    received = exchange(direct, count, backs)

    correction = pl.pallas_call(
        lambda *refs: gather_kernel(direct, count, slots, rows, *refs),
        out_shape=jax.ShapeDtypeStruct((slots, rows, voxels), jnp.float32),
        in_specs=[SMEM, SMEM] + [VMEM] * len(received),
        out_specs=VMEM,
        scratch_shapes=[
            pltpu.VMEM((2 * SPREAD * rows, half), jnp.float32),
            pltpu.VMEM((2, half), jnp.float32),
        ],
        compiler_params=params(16),
        name="gather",
    )(offsets_here, counts_here, *received)
    return residual[None], correction


def solution(mesh):
    placed = (P("tile", "row", None), P("tile", "row", None), P("tile", None, None), P(), P())
    return jax.shard_map(
        local,
        mesh=mesh,
        in_specs=placed,
        out_specs=(P("tile", "row", None), P("tile", "row", None)),
        check_vma=False,
    )
```

```python
import jax
import jax.numpy as jnp
import numpy as np
from jax import lax
from jax.experimental import pallas as pl
from jax.experimental.pallas import tpu as pltpu
from jax.sharding import PartitionSpec as P


SPREAD = 4
RIM = 3
HALO = 8
GROUP = 22
TERMS = 2
FIRST = 3
DIRECT_LIMIT = 16
EXTRA_ROWS = 8
SUM_SCALE = 2048.0
LOW_SCALE = 32000.0
CODE_TOP = 32000.0

decay_length = 2.0
row_floor = 0.5


SMEM = pl.BlockSpec(memory_space=pltpu.SMEM)
VMEM = pl.BlockSpec(memory_space=pltpu.VMEM)
HBM = pl.BlockSpec(memory_space=pltpu.HBM)


def params(mib):
    return pltpu.CompilerParams(vmem_limit_bytes=mib << 20)


def smoothing_taps():
    spread_taps = np.exp(-np.abs(np.arange(-RIM, RIM + 1)) / decay_length)
    return spread_taps / spread_taps.sum()


def each_piece(direct, count, member, refs, body):
    if direct:
        for k in range(count):
            body(refs[k], member ^ k)
    else:

        def step(k, carry):
            body(refs[0].at[k], k)
            return carry

        lax.fori_loop(0, count, step, 0)


def group_start(offsets, angle, group, slots):
    low = offsets[angle, group * slots]
    for j in range(1, slots):
        low = jnp.minimum(low, offsets[angle, group * slots + j])
    return low


def load_kernel(direct, count, slots, offsets_in, count_in, volume_in, table_in, intensity, *refs):
    lists = count if direct else 1
    near_rows, far_rows, table_out, offsets_out, count_out = refs[:5]
    pieces = refs[5 : 5 + lists]
    offsets, tile_count, volume, sems = refs[5 + lists :]
    member = lax.axis_index("tile")
    even = lax.rem(lax.axis_index("row"), 2) == 0
    last = intensity.shape[0] - HALO
    first_copy = pltpu.make_async_copy(offsets_in, offsets, sems.at[0])
    count_copy = pltpu.make_async_copy(count_in, tile_count, sems.at[1])
    volume_copy = pltpu.make_async_copy(volume_in, volume, sems.at[2])
    near = pl.multiple_of(jnp.where(even, last, 0), HALO)
    far = pl.multiple_of(jnp.where(even, 0, last), HALO)
    near_copy = pltpu.make_async_copy(intensity.at[pl.ds(near, HALO)], near_rows, sems.at[3])
    far_copy = pltpu.make_async_copy(intensity.at[pl.ds(far, HALO)], far_rows, sems.at[4])
    later = [near_copy, far_copy]
    for i, (here, there) in enumerate(
        ((table_in, table_out), (offsets_in, offsets_out), (count_in, count_out))
    ):
        later.append(pltpu.make_async_copy(here, there, sems.at[5 + i]))
    first_copy.start()
    count_copy.start()
    volume_copy.start()
    for copy in later:
        copy.start()
    first_copy.wait()
    count_copy.wait()
    live = tile_count[member]
    volume_copy.wait()

    def one(piece, angle):
        start = group_start(offsets, angle, member, slots)
        places = [offsets[angle, member * slots + j] - start for j in range(slots)]
        places = [jnp.where(j < live, places[j], -1) for j in range(slots)]
        for s in range(SPREAD):
            total = jnp.zeros(volume.shape[1:], jnp.float32)
            for j in range(slots):
                total = total + jnp.where(places[j] == s, 1.0, 0.0) * volume[j]
            piece[s] = total.astype(piece.dtype)

    each_piece(direct, count, member, pieces, one)
    for copy in later:
        copy.wait()


def tables(slots, blocks, offset_rows, tile_count, table, inverse, sums):
    member = lax.axis_index("tile")
    half = table.shape[1] // 2
    padded = inverse.shape[0]
    total = offset_rows.shape[1]
    by_column = jnp.sum(table.astype(jnp.float32), axis=0, keepdims=True)
    mine = offset_rows[pl.ds(member, 1), :]
    lane = lax.broadcasted_iota(jnp.int32, (1, total), 1)
    alive = jnp.zeros((1, total), jnp.float32)
    for g in range(total // slots):
        here = (lane >= g * slots) & (lane < g * slots + tile_count[g])
        alive = jnp.where(here, 1.0, alive)
    block = lax.broadcasted_iota(jnp.int32, (padded, total), 0)
    hits = jnp.where(block == mine, alive, 0.0)
    counts = jnp.sum(hits, axis=1, keepdims=True)
    before = jnp.sum(jnp.where(block == mine + 1, alive, 0.0), axis=1, keepdims=True)
    rows = counts * by_column[:, :half] + before * by_column[:, half:]
    inside = lax.broadcasted_iota(jnp.int32, (padded, half), 0) < blocks
    inverse[...] = jnp.where(inside, 1.0 / jnp.maximum(rows, row_floor), 0.0)
    ones = jnp.ones((8, table.shape[1]), table.dtype)
    by_voxel = lax.dot_general(
        ones, table, (((1,), (1,)), ((), ())), preferred_element_type=jnp.float32
    )[0:1]
    scaled = by_voxel * SUM_SCALE
    whole = jnp.floor(scaled)
    low = jnp.floor((scaled - whole) * LOW_SCALE + 0.5)
    packed = jnp.concatenate(
        [whole[:, :half], whole[:, half:], low[:, :half], low[:, half:]], axis=0
    )
    sums[...] = jnp.concatenate([packed, jnp.zeros((4, half), jnp.float32)], axis=0)


def tap_matrix(half, terms):
    place = np.arange(4 * half)[:, None] - half
    apart = np.abs(place - np.arange(2 * half)[None, :])
    taps = smoothing_taps()
    rest = np.where(apart <= RIM, np.exp(-apart / decay_length) * taps[RIM], 0.0)
    parts = []
    for _ in range(terms):
        part = rest.astype(jnp.bfloat16)
        parts.append(part)
        rest = rest - part.astype(np.float64)
    return np.concatenate(parts, axis=0)


def phase_kernel(slots, tile_count, offset_rows, intensity, near_rows, far_rows, footprint, *refs):
    taps, phase, inverse, sums, padded, across = refs
    rows, columns = intensity.shape
    half = footprint.shape[1] // 2
    blocks = columns // half
    tables(slots, blocks, offset_rows, tile_count, footprint[...], inverse, sums)
    even = lax.rem(lax.axis_index("row"), 2) == 0
    decay = float(np.exp(-1.0 / decay_length))
    centre = float(smoothing_taps()[RIM])
    tall = rows + 2 * HALO
    edge = jnp.zeros((tall, half), padded.dtype)
    padded[:, :half] = edge
    padded[:, half + columns :] = edge
    inner = slice(half, half + columns)
    padded[HALO : HALO + rows, inner] = intensity[...]
    near = near_rows[...].astype(jnp.float32)
    far = far_rows[...].astype(jnp.float32)
    padded[:HALO, inner] = jnp.where(even, far, near).astype(padded.dtype)
    padded[HALO + rows :, inner] = jnp.where(even, near, far).astype(padded.dtype)
    terms = taps.shape[0] // (4 * half)
    pairs = blocks // 2
    group = max(d for d in range(1, min(GROUP, pairs) + 1) if pairs % d == 0)
    stride = rows // 8

    def step(g, carry):
        tiles = [
            padded[:, pl.ds(pl.multiple_of((g * group + i) * 2 * half, half), 4 * half)]
            for i in range(group)
        ]
        stacked = jnp.concatenate([jnp.concatenate(tiles, axis=0)] * terms, axis=1)
        filtered = jnp.dot(stacked, taps[...], preferred_element_type=jnp.float32)
        for i in range(group):
            for h in range(2):
                across[(g * group + i) * 2 + h] = filtered[
                    i * tall : (i + 1) * tall, h * half : (h + 1) * half
                ]
        for i in range(2 * group):
            block = g * 2 * group + i
            lines = [
                across[block, pl.ds(HALO - RIM + m, 8, stride=stride), :]
                for m in range(stride + 2 * RIM)
            ]
            for k in range(stride):
                mid = k + RIM
                total = lines[mid - RIM] + lines[mid + RIM]
                for m in range(RIM - 1, 0, -1):
                    total = total * decay + (lines[mid - m] + lines[mid + m])
                total = total * decay + lines[mid]
                phase[block, pl.ds(k, 8, stride=stride), :] = -jnp.log(total * centre)
        return carry

    lax.fori_loop(0, pairs // group, step, 0)


def write_kernel(residual, out):
    blocks, _, half = residual.shape
    for block in range(blocks):
        out[:, block * half : (block + 1) * half] = residual[block]


def encode(window, table, sums, piece):
    rows = window.shape[0]
    half = table.shape[1] // 2
    stacked = jnp.concatenate(
        [window[:, s * half : (s + 2) * half] for s in range(SPREAD)], axis=0
    )
    back = lax.dot_general(
        stacked, table, (((1,), (1,)), ((), ())), preferred_element_type=jnp.float32
    )
    top = jnp.max(jnp.max(jnp.abs(back), axis=0, keepdims=True), axis=1, keepdims=True)
    power = jnp.floor(jnp.log2(CODE_TOP / jnp.maximum(top, 1e-30)))
    code = jnp.round(back * jnp.exp2(power)).astype(jnp.int32)
    for s in range(SPREAD):
        for h in range(2):
            base = (2 * s + h) * rows
            piece[base : base + rows, :] = code[
                s * rows : (s + 1) * rows, h * half : (h + 1) * half
            ].astype(piece.dtype)
    base = 2 * SPREAD * rows
    line = lax.broadcasted_iota(jnp.int32, (EXTRA_ROWS, half), 0)
    extra = jnp.where(line < 4, sums, jnp.broadcast_to(power, (EXTRA_ROWS, half)))
    piece[base : base + EXTRA_ROWS, :] = extra.astype(jnp.int32).astype(piece.dtype)


def angle_kernel(direct, count, slots, first, offsets, phase, footprint, inverse, sums, *refs):
    lists = count if direct else 1
    arrived, residual, windows, sent = refs[:lists], refs[lists], refs[lists + 1], refs[lists + 2 :]
    member = lax.axis_index("tile")
    table = footprint[...]
    blocks, rows, half = phase.shape
    voxels = footprint.shape[0]

    def subtract(piece, group):
        start = group_start(offsets, member, group, slots)
        image = jnp.dot(
            piece[...].reshape(SPREAD * rows, voxels), table, preferred_element_type=jnp.float32
        )
        for s in range(SPREAD + 1):
            part = None
            if s < SPREAD:
                part = image[s * rows : (s + 1) * rows, :half]
            if s > 0:
                far = image[(s - 1) * rows : s * rows, half:]
                part = far if part is None else part + far
            block = start + s
            if s == SPREAD:
                part = jnp.where(block < blocks, part, 0.0)
                block = jnp.minimum(block, blocks - 1)
            residual[block] = residual[block] - part

    each_piece(direct, count, member, arrived, subtract)

    def weigh(window, group):
        start = group_start(offsets, member, group, slots)
        for s in range(SPREAD + 1):
            block = jnp.minimum(start + s, blocks - 1)
            scale = inverse[pl.ds(start + s, 1), :]
            window[:, s * half : (s + 1) * half] = (residual[block] * scale).astype(window.dtype)

    if direct:
        for k in first:
            weigh(windows.at[k], member ^ k)
        for piece, k in zip(sent, first):
            encode(windows[k], table, sums[...], piece)
        for k in range(count):
            if k not in first:
                weigh(windows.at[k], member ^ k)
    else:

        def step(k, carry):
            weigh(windows.at[k], k)
            encode(windows[k], table, sums[...], sent[0].at[k])
            return carry

        lax.fori_loop(0, count, step, 0)


def back_kernel(ks, windows, footprint, sums, *sent):
    for piece, k in zip(sent, ks):
        encode(windows[k], footprint[...], sums[...], piece)


def gather_kernel(direct, ks, slots, rows, last, offsets, tile_count, *refs):
    lists = len(ks) if direct else 1
    received = refs[:lists]
    refs = refs[lists:]
    earlier = None
    if direct and last:
        earlier, earlier_sums, refs = refs[0], refs[1], refs[2:]
    correction, column_sums, decoded = refs
    member = lax.axis_index("tile")
    live = tile_count[member]
    half = column_sums.shape[1]
    base = 2 * SPREAD * rows

    def unpack(piece, into):
        extra = piece[base : base + EXTRA_ROWS, :].astype(jnp.float32)
        into[...] = piece[0:base, :].astype(jnp.float32) * jnp.exp2(-extra[4:5])
        return (extra[0:2] + extra[2:4] * (1.0 / LOW_SCALE)) * (1.0 / SUM_SCALE)

    def block_of(into, angle, start, j):
        at = (offsets[angle, member * slots + j] - start) * (2 * rows)
        return into[pl.ds(pl.multiple_of(at, 2 * rows), 2 * rows), :]

    if direct:
        total = earlier_sums[0:2] if last else jnp.zeros((2, half), jnp.float32)
        angles = [member ^ k for k in ks]
        starts = []
        for i, piece in enumerate(received):
            total = total + unpack(piece, decoded.at[i])
            starts.append(group_start(offsets, angles[i], member, slots))
    else:
        column_sums[...] = jnp.zeros_like(column_sums)
        correction[...] = jnp.zeros_like(correction)

        def step(k, carry):
            column_sums[0:2] += unpack(received[0].at[k], decoded.at[0])
            start = group_start(offsets, k, member, slots)
            for j in range(slots):
                correction[j] += block_of(decoded.at[0], k, start, j)
            return carry

        lax.fori_loop(0, len(ks), step, 0)
        total = column_sums[0:2]

    if last:
        inverse = 1.0 / total
    else:
        column_sums[0:2] = total
    for j in range(slots):
        if direct:
            sum_here = earlier[j] if last else None
            for i, angle in enumerate(angles):
                part = block_of(decoded.at[i], angle, starts[i], j)
                sum_here = part if sum_here is None else sum_here + part
        else:
            sum_here = correction[j]
        if not last:
            correction[j] = sum_here
        elif direct:
            weight = jnp.where(j < live, 1.0, 0.0)
            for h in range(2):
                correction[j, :, h * half : (h + 1) * half] = sum_here[
                    h * rows : (h + 1) * rows
                ] * (inverse[h : h + 1] * weight)
        else:
            weight = jnp.where(j < live, 1.0, 0.0)
            correction[j] = sum_here * weight * jnp.concatenate(
                [jnp.broadcast_to(inverse[h : h + 1], (rows, half)) for h in range(2)], axis=0
            )


def exchange(direct, count, pieces):
    if not direct:
        return [lax.all_to_all(pieces[0], "tile", split_axis=0, concat_axis=0, tiled=True)]
    arrived = [pieces[0]]
    for k in range(1, count):
        arrived.append(lax.ppermute(pieces[k], "tile", [(i, i ^ k) for i in range(count)]))
    return arrived


def swap_halos(near_rows, far_rows):
    count = lax.axis_size("row")
    pairs = [(i, i + 1) for i in range(0, count - 1, 2)]
    between = [(i, i + 1) for i in range(1, count - 1, 2)]
    far_rows = lax.ppermute(far_rows, "row", between + [(b, a) for a, b in between])
    near_rows = lax.ppermute(near_rows, "row", pairs + [(b, a) for a, b in pairs])
    return near_rows, far_rows


def use_direct(count):
    return count <= DIRECT_LIMIT and count & (count - 1) == 0


def local(intensity, volume, footprint, foot_offset, tile_count):
    count = lax.axis_size("tile")
    direct = use_direct(count)
    slots, rows, voxels = volume.shape
    angles_here, _, window = footprint.shape
    assert angles_here == 1
    half = window // 2
    columns = intensity.shape[2]
    blocks = columns // half
    padded_blocks = -(-(blocks + SPREAD + 1) // 8) * 8
    offsets = jnp.transpose(foot_offset)
    table = footprint[0]

    def piece_shapes(shape, dtype):
        if direct:
            return [jax.ShapeDtypeStruct(shape, dtype)] * count
        return [jax.ShapeDtypeStruct((count,) + shape, dtype)]

    halo_shape = jax.ShapeDtypeStruct((HALO, columns), intensity.dtype)
    load_shapes = piece_shapes((SPREAD, rows, voxels), jnp.bfloat16)
    near_rows, far_rows, table, offsets_here, counts_here, *loads = pl.pallas_call(
        lambda *refs: load_kernel(direct, count, slots, *refs),
        out_shape=[halo_shape, halo_shape]
        + [jax.ShapeDtypeStruct(x.shape, x.dtype) for x in (table, offsets, tile_count)]
        + load_shapes,
        in_specs=[HBM] * 5,
        out_specs=[VMEM] * (5 + len(load_shapes)),
        scratch_shapes=[
            pltpu.SMEM(offsets.shape, jnp.int32),
            pltpu.SMEM(tile_count.shape, jnp.int32),
            pltpu.VMEM(volume.shape, volume.dtype),
            pltpu.SemaphoreType.DMA((8,)),
        ],
        compiler_params=params(16),
        name="loads",
    )(*[pltpu.with_memory_space_constraint(x, pltpu.HBM) for x in (offsets, tile_count, volume, table, intensity[0])])
    near_rows, far_rows = swap_halos(near_rows, far_rows)
    arrived = exchange(direct, count, loads)

    taps = jnp.asarray(tap_matrix(half, TERMS))
    tall = rows + 2 * HALO
    phase_map, inverse, sums = pl.pallas_call(
        lambda *refs: phase_kernel(slots, *refs),
        out_shape=[
            jax.ShapeDtypeStruct((blocks, rows, half), jnp.float32),
            jax.ShapeDtypeStruct((padded_blocks, half), jnp.float32),
            jax.ShapeDtypeStruct((EXTRA_ROWS, half), jnp.float32),
        ],
        in_specs=[SMEM] + [VMEM] * 6,
        out_specs=[VMEM] * 3,
        scratch_shapes=[
            pltpu.VMEM((tall, columns + 2 * half), intensity.dtype),
            pltpu.VMEM((blocks, tall, half), jnp.float32),
        ],
        compiler_params=params(16),
        name="phase",
    )(counts_here, offsets_here, intensity[0], near_rows, far_rows, table, taps)

    piece_shape = (2 * SPREAD * rows + EXTRA_ROWS, half)
    one_piece = jax.ShapeDtypeStruct(piece_shape, jnp.int16)
    first = list(range(count - 1, 0, -1))[:FIRST] if direct else []
    rest = [k for k in range(count) if k not in first]
    sent_shapes = [one_piece] * len(first) if direct else piece_shapes(piece_shape, jnp.int16)
    residual, windows, *sent = pl.pallas_call(
        lambda *refs: angle_kernel(direct, count, slots, first, *refs),
        out_shape=[
            jax.ShapeDtypeStruct((blocks, rows, half), jnp.float32),
            jax.ShapeDtypeStruct((count, rows, (SPREAD + 1) * half), jnp.bfloat16),
        ]
        + sent_shapes,
        in_specs=[SMEM] + [VMEM] * (4 + len(arrived)),
        out_specs=[VMEM] * (2 + len(sent_shapes)),
        input_output_aliases={1: 0},
        compiler_params=params(16),
        name="angle",
    )(offsets_here, phase_map, table, inverse, sums, *arrived)
    if direct:
        others = pl.pallas_call(
            lambda *refs: back_kernel(rest, *refs),
            out_shape=[one_piece] * len(rest),
            in_specs=[VMEM] * 3,
            out_specs=[VMEM] * len(rest),
            compiler_params=params(16),
            name="back",
        )(windows, table, sums)
        by_partner = dict(zip(first + rest, [*sent, *others]))
        sent = [by_partner[k] for k in range(count)]
    received = exchange(direct, count, sent)

    residual = pl.pallas_call(
        write_kernel,
        out_shape=jax.ShapeDtypeStruct((rows, columns), jnp.float32),
        in_specs=[VMEM],
        out_specs=VMEM,
        compiler_params=params(16),
        name="write",
    )(residual)

    def gather(ks, pieces, last, *earlier):
        flat = (slots, 2 * rows, half)
        shape = (slots, rows, voxels) if direct and last else flat
        return pl.pallas_call(
            lambda *refs: gather_kernel(direct, ks, slots, rows, last, *refs),
            out_shape=[
                jax.ShapeDtypeStruct(shape, jnp.float32),
                jax.ShapeDtypeStruct((8, half), jnp.float32),
            ],
            in_specs=[SMEM, SMEM] + [VMEM] * (len(pieces) + len(earlier)),
            out_specs=[VMEM, VMEM],
            scratch_shapes=[
                pltpu.VMEM((len(pieces), 2 * SPREAD * rows, half), jnp.float32),
            ],
            compiler_params=params(16),
            name="gather_last" if last else "gather_first",
        )(offsets_here, counts_here, *pieces, *earlier)

    if direct:
        near = list(range(count // 2))
        far = list(range(count // 2, count))
        partial = gather(near, received[: count // 2], False)
        correction = gather(far, received[count // 2 :], True, *partial)[0]
    else:
        flat = gather(list(range(count)), received, True)[0]
        correction = jnp.swapaxes(flat.reshape(slots, 2, rows, half), 1, 2)
        correction = correction.reshape(slots, rows, voxels)
    return residual[None], correction


def solution(mesh):
    placed = (P("tile", "row", None), P("tile", "row", None), P("tile", None, None), P(), P())
    return jax.shard_map(
        local,
        mesh=mesh,
        in_specs=placed,
        out_specs=(P("tile", "row", None), P("tile", "row", None)),
        check_vma=False,
    )
```

```python
import jax
import jax.numpy as jnp
import numpy as np
from jax import lax
from jax.experimental import pallas as pl
from jax.experimental.pallas import tpu as pltpu
from jax.sharding import PartitionSpec as P


SPREAD = 4
RIM = 3
HALO = 8
GROUP = 22
TERMS = 2
FIRST = 1
DIRECT_LIMIT = 16
EXTRA_ROWS = 8
SUM_SCALE = 2048.0
LOW_SCALE = 32000.0
CODE_TOP = 32000.0

decay_length = 2.0
row_floor = 0.5


SMEM = pl.BlockSpec(memory_space=pltpu.SMEM)
VMEM = pl.BlockSpec(memory_space=pltpu.VMEM)
HBM = pl.BlockSpec(memory_space=pltpu.HBM)


def params(mib):
    return pltpu.CompilerParams(vmem_limit_bytes=mib << 20)


def smoothing_taps():
    spread_taps = np.exp(-np.abs(np.arange(-RIM, RIM + 1)) / decay_length)
    return spread_taps / spread_taps.sum()


def each_piece(direct, count, member, refs, body):
    if direct:
        for k in range(count):
            body(refs[k], member ^ k)
    else:

        def step(k, carry):
            body(refs[0].at[k], k)
            return carry

        lax.fori_loop(0, count, step, 0)


def group_start(offsets, angle, group, slots):
    low = offsets[angle, group * slots]
    for j in range(1, slots):
        low = jnp.minimum(low, offsets[angle, group * slots + j])
    return low


def load_kernel(
    direct, count, slots, offsets_in, count_in, volume_in, table_in, taps_in, intensity, *refs
):
    lists = count if direct else 1
    near_rows, far_rows, table_out, taps_out, alive = refs[:5]
    pieces = refs[5 : 5 + lists]
    offsets, tile_count, volume, sems = refs[5 + lists :]
    member = lax.axis_index("tile")
    even = lax.rem(lax.axis_index("row"), 2) == 0
    last = intensity.shape[0] - HALO
    first_copy = pltpu.make_async_copy(offsets_in, offsets, sems.at[0])
    count_copy = pltpu.make_async_copy(count_in, tile_count, sems.at[1])
    near = pl.multiple_of(jnp.where(even, last, 0), HALO)
    far = pl.multiple_of(jnp.where(even, 0, last), HALO)
    near_copy = pltpu.make_async_copy(intensity.at[pl.ds(near, HALO)], near_rows, sems.at[3])
    far_copy = pltpu.make_async_copy(intensity.at[pl.ds(far, HALO)], far_rows, sems.at[4])
    later = [near_copy, far_copy]
    for i, (here, there) in enumerate(
        ((table_in, table_out), (taps_in, taps_out))
    ):
        later.append(pltpu.make_async_copy(here, there, sems.at[5 + i]))
    volume_copies = [
        pltpu.make_async_copy(volume_in.at[j], volume.at[j], sems.at[8 + j]) for j in range(slots)
    ]
    for copy in volume_copies:
        copy.start()
    first_copy.start()
    count_copy.start()
    for copy in later:
        copy.start()
    first_copy.wait()
    count_copy.wait()
    live = tile_count[member]
    for copy in volume_copies:
        copy.wait()

    def one(piece, angle):
        start = group_start(offsets, angle, member, slots)
        places = [offsets[angle, member * slots + j] - start for j in range(slots)]
        places = [jnp.where(j < live, places[j], -1) for j in range(slots)]
        for s in range(SPREAD):
            total = jnp.zeros(volume.shape[1:], jnp.float32)
            for j in range(slots):
                total = total + jnp.where(places[j] == s, 1.0, 0.0) * volume[j]
            piece[s] = total.astype(piece.dtype)

    each_piece(direct, count, member, pieces, one)
    lane = lax.broadcasted_iota(jnp.int32, alive.shape, 1)
    flags = jnp.zeros(alive.shape, jnp.float32)
    for g in range(alive.shape[1] // slots):
        here = (lane >= g * slots) & (lane < g * slots + tile_count[g])
        flags = jnp.where(here, 1.0, flags)
    alive[...] = flags
    for copy in later:
        copy.wait()


def tables(slots, blocks, offset_rows, alive, table, inverse, sums, starts):
    member = lax.axis_index("tile")
    half = table.shape[1] // 2
    padded = inverse.shape[0]
    total = offset_rows.shape[1]
    by_column = jnp.sum(table.astype(jnp.float32), axis=0, keepdims=True)
    mine = offset_rows[pl.ds(member, 1), :]
    group = lax.broadcasted_iota(jnp.int32, (starts.shape[0], total), 0)
    lane = lax.broadcasted_iota(jnp.int32, (starts.shape[0], total), 1)
    own = (lane >= group * slots) & (lane < (group + 1) * slots)
    lowest = jnp.min(jnp.where(own, mine, 1 << 20), axis=1, keepdims=True)
    starts[...] = jnp.broadcast_to(lowest, starts.shape)
    alive = alive[0:1, :]
    block = lax.broadcasted_iota(jnp.int32, (padded, total), 0)
    hits = jnp.where(block == mine, alive, 0.0)
    counts = jnp.sum(hits, axis=1, keepdims=True)
    before = jnp.sum(jnp.where(block == mine + 1, alive, 0.0), axis=1, keepdims=True)
    rows = counts * by_column[:, :half] + before * by_column[:, half:]
    inside = lax.broadcasted_iota(jnp.int32, (padded, half), 0) < blocks
    inverse[...] = jnp.where(inside, 1.0 / jnp.maximum(rows, row_floor), 0.0)
    ones = jnp.ones((8, table.shape[1]), table.dtype)
    by_voxel = lax.dot_general(
        ones, table, (((1,), (1,)), ((), ())), preferred_element_type=jnp.float32
    )[0:1]
    scaled = by_voxel * SUM_SCALE
    whole = jnp.floor(scaled)
    low = jnp.floor((scaled - whole) * LOW_SCALE + 0.5)
    packed = jnp.concatenate(
        [whole[:, :half], whole[:, half:], low[:, :half], low[:, half:]], axis=0
    )
    sums[...] = jnp.concatenate([packed, jnp.zeros((4, half), jnp.float32)], axis=0)


def tap_matrix(half, terms):
    place = np.arange(4 * half)[:, None] - half
    apart = np.abs(place - np.arange(2 * half)[None, :])
    taps = smoothing_taps()
    rest = np.where(apart <= RIM, np.exp(-apart / decay_length) * taps[RIM], 0.0)
    parts = []
    for _ in range(terms):
        part = rest.astype(jnp.bfloat16)
        parts.append(part)
        rest = rest - part.astype(np.float64)
    return np.concatenate(parts, axis=0)


def phase_kernel(slots, alive, offset_rows, intensity, near_rows, far_rows, footprint, *refs):
    taps, phase, inverse, sums, starts, padded, across = refs
    rows, columns = intensity.shape
    half = footprint.shape[1] // 2
    blocks = columns // half
    even = lax.rem(lax.axis_index("row"), 2) == 0
    decay = float(np.exp(-1.0 / decay_length))
    centre = float(smoothing_taps()[RIM])
    tall = rows + 2 * HALO
    edge = jnp.zeros((tall, half), padded.dtype)
    padded[:, :half] = edge
    padded[:, half + columns :] = edge
    inner = slice(half, half + columns)
    padded[HALO : HALO + rows, inner] = intensity[...]
    near = near_rows[...].astype(jnp.float32)
    far = far_rows[...].astype(jnp.float32)
    padded[:HALO, inner] = jnp.where(even, far, near).astype(padded.dtype)
    padded[HALO + rows :, inner] = jnp.where(even, near, far).astype(padded.dtype)
    tables(slots, blocks, offset_rows, alive, footprint[...], inverse, sums, starts)
    terms = taps.shape[0] // (4 * half)
    pairs = blocks // 2
    group = max(d for d in range(1, min(GROUP, pairs) + 1) if pairs % d == 0)
    stride = rows // 8

    def step(g, carry):
        tiles = [
            padded[:, pl.ds(pl.multiple_of((g * group + i) * 2 * half, half), 4 * half)]
            for i in range(group)
        ]
        stacked = jnp.concatenate([jnp.concatenate(tiles, axis=0)] * terms, axis=1)
        filtered = jnp.dot(stacked, taps[...], preferred_element_type=jnp.float32)
        for i in range(group):
            for h in range(2):
                across[(g * group + i) * 2 + h] = filtered[
                    i * tall : (i + 1) * tall, h * half : (h + 1) * half
                ]
        for i in range(2 * group):
            block = g * 2 * group + i
            lines = [
                across[block, pl.ds(HALO - RIM + m, 8, stride=stride), :]
                for m in range(stride + 2 * RIM)
            ]
            for k in range(stride):
                mid = k + RIM
                total = lines[mid - RIM] + lines[mid + RIM]
                for m in range(RIM - 1, 0, -1):
                    total = total * decay + (lines[mid - m] + lines[mid + m])
                total = total * decay + lines[mid]
                phase[block, pl.ds(k, 8, stride=stride), :] = -jnp.log(total * centre)
        return carry

    lax.fori_loop(0, pairs // group, step, 0)


def write_kernel(count, slots, offsets, tile_count, residual, out, plan):
    member = lax.axis_index("tile")
    lane = lax.broadcasted_iota(jnp.int32, (1, plan.shape[1]), 1)

    def one(angle, carry):
        start = group_start(offsets, angle, member, slots)
        row = jnp.zeros((1, plan.shape[1]), jnp.int32)
        for j in range(slots):
            row = jnp.where(lane == j, offsets[angle, member * slots + j] - start, row)
        plan[pl.ds(angle, 1), :] = row
        return carry

    lax.fori_loop(0, count, one, 0)
    plan[count : count + 1, :] = (lane < tile_count[member]).astype(jnp.int32)
    blocks, _, half = residual.shape
    for block in range(blocks):
        out[:, block * half : (block + 1) * half] = residual[block]


def encode(window, table, sums, piece):
    rows = window.shape[0]
    half = table.shape[1] // 2
    stacked = jnp.concatenate(
        [window[:, s * half : (s + 2) * half] for s in range(SPREAD)], axis=0
    )
    back = lax.dot_general(
        stacked, table, (((1,), (1,)), ((), ())), preferred_element_type=jnp.float32
    )
    top = jnp.max(jnp.max(jnp.abs(back), axis=0, keepdims=True), axis=1, keepdims=True)
    power = jnp.floor(jnp.log2(CODE_TOP / jnp.maximum(top, 1e-30)))
    code = jnp.round(back * jnp.exp2(power)).astype(jnp.int32)
    for s in range(SPREAD):
        for h in range(2):
            base = (2 * s + h) * rows
            piece[base : base + rows, :] = code[
                s * rows : (s + 1) * rows, h * half : (h + 1) * half
            ].astype(piece.dtype)
    base = 2 * SPREAD * rows
    line = lax.broadcasted_iota(jnp.int32, (EXTRA_ROWS, half), 0)
    extra = jnp.where(line < 4, sums, jnp.broadcast_to(power, (EXTRA_ROWS, half)))
    piece[base : base + EXTRA_ROWS, :] = extra.astype(jnp.int32).astype(piece.dtype)


def angle_kernel(
    direct, count, first, starts, phase, footprint, inverse, sums, *refs
):
    lists = count if direct else 1
    arrived, residual, windows = refs[:lists], refs[lists], refs[lists + 1]
    sent, images = refs[lists + 2 : -1], refs[-1]
    member = lax.axis_index("tile")
    table = footprint[...]
    blocks, rows, half = phase.shape
    voxels = footprint.shape[0]

    def project(piece, image):
        image[...] = jnp.dot(
            piece[...].reshape(SPREAD * rows, voxels), table, preferred_element_type=jnp.float32
        )

    def subtract(image, group):
        start = starts[group, 0]
        for s in range(SPREAD + 1):
            part = None
            if s < SPREAD:
                part = image[s * rows : (s + 1) * rows, :half]
            if s > 0:
                far = image[(s - 1) * rows : s * rows, half:]
                part = far if part is None else part + far
            block = start + s
            if s == SPREAD:
                part = jnp.where(block < blocks, part, 0.0)
                block = jnp.minimum(block, blocks - 1)
            residual[block] = residual[block] - part

    if direct:
        for k in range(count):
            project(arrived[k], images.at[k])
        for k in range(count):
            subtract(images.at[k], member ^ k)
    else:

        def one(k, carry):
            project(arrived[0].at[k], images.at[0])
            subtract(images.at[0], k)
            return carry

        lax.fori_loop(0, count, one, 0)

    def weigh(window, group):
        start = starts[group, 0]
        for s in range(SPREAD + 1):
            block = jnp.minimum(start + s, blocks - 1)
            scale = inverse[pl.ds(start + s, 1), :]
            window[:, s * half : (s + 1) * half] = (residual[block] * scale).astype(window.dtype)

    if direct:
        for k in first:
            weigh(windows.at[k], member ^ k)
        for piece, k in zip(sent, first):
            encode(windows[k], table, sums[...], piece)
        for k in range(count):
            if k not in first:
                weigh(windows.at[k], member ^ k)
    else:

        def step(k, carry):
            weigh(windows.at[k], k)
            encode(windows[k], table, sums[...], sent[0].at[k])
            return carry

        lax.fori_loop(0, count, step, 0)


def back_kernel(ks, windows, footprint, sums, *sent):
    for piece, k in zip(sent, ks):
        encode(windows[k], footprint[...], sums[...], piece)


def gather_kernel(direct, count, ks, slots, rows, last, plan, *refs):
    lists = len(ks) if direct else 1
    received = refs[:lists]
    refs = refs[lists:]
    earlier = None
    if direct and last:
        earlier, earlier_sums, refs = refs[0], refs[1], refs[2:]
    correction, column_sums, decoded = refs
    member = lax.axis_index("tile")
    half = column_sums.shape[1]
    base = 2 * SPREAD * rows

    def unpack(piece, into):
        extra = piece[base : base + EXTRA_ROWS, :].astype(jnp.float32)
        into[...] = piece[0:base, :].astype(jnp.float32) * jnp.exp2(-extra[4:5])
        return (extra[0:2] + extra[2:4] * (1.0 / LOW_SCALE)) * (1.0 / SUM_SCALE)

    def block_of(into, angle, j):
        at = plan[angle, j] * (2 * rows)
        return into[pl.ds(pl.multiple_of(at, 2 * rows), 2 * rows), :]

    if direct:
        total = earlier_sums[0:2] if last else jnp.zeros((2, half), jnp.float32)
        angles = [member ^ k for k in ks]
        for i, piece in enumerate(received):
            total = total + unpack(piece, decoded.at[i])
    else:
        column_sums[...] = jnp.zeros_like(column_sums)
        correction[...] = jnp.zeros_like(correction)

        def step(k, carry):
            column_sums[0:2] += unpack(received[0].at[k], decoded.at[0])
            for j in range(slots):
                correction[j] += block_of(decoded.at[0], k, j)
            return carry

        lax.fori_loop(0, len(ks), step, 0)
        total = column_sums[0:2]

    if last:
        inverse = 1.0 / total
    else:
        column_sums[0:2] = total
    for j in range(slots):
        if direct:
            sum_here = earlier[j] if last else None
            for i, angle in enumerate(angles):
                part = block_of(decoded.at[i], angle, j)
                sum_here = part if sum_here is None else sum_here + part
        else:
            sum_here = correction[j]
        if not last:
            correction[j] = sum_here
        elif direct:
            weight = jnp.where(plan[count, j] > 0, 1.0, 0.0)
            for h in range(2):
                correction[j, :, h * half : (h + 1) * half] = sum_here[
                    h * rows : (h + 1) * rows
                ] * (inverse[h : h + 1] * weight)
        else:
            weight = jnp.where(plan[count, j] > 0, 1.0, 0.0)
            correction[j] = sum_here * weight * jnp.concatenate(
                [jnp.broadcast_to(inverse[h : h + 1], (rows, half)) for h in range(2)], axis=0
            )


def exchange(direct, count, pieces):
    if not direct:
        return [lax.all_to_all(pieces[0], "tile", split_axis=0, concat_axis=0, tiled=True)]
    arrived = [pieces[0]]
    for k in range(1, count):
        arrived.append(lax.ppermute(pieces[k], "tile", [(i, i ^ k) for i in range(count)]))
    return arrived


def swap_halos(near_rows, far_rows):
    count = lax.axis_size("row")
    pairs = [(i, i + 1) for i in range(0, count - 1, 2)]
    between = [(i, i + 1) for i in range(1, count - 1, 2)]
    far_rows = lax.ppermute(far_rows, "row", between + [(b, a) for a, b in between])
    near_rows = lax.ppermute(near_rows, "row", pairs + [(b, a) for a, b in pairs])
    return near_rows, far_rows


def use_direct(count):
    return count <= DIRECT_LIMIT and count & (count - 1) == 0


def local(intensity, volume, footprint, foot_offset, tile_count):
    count = lax.axis_size("tile")
    direct = use_direct(count)
    slots, rows, voxels = volume.shape
    angles_here, _, window = footprint.shape
    assert angles_here == 1
    half = window // 2
    columns = intensity.shape[2]
    blocks = columns // half
    padded_blocks = -(-(blocks + SPREAD + 1) // 8) * 8
    offsets = jnp.transpose(foot_offset)
    table = footprint[0]

    def piece_shapes(shape, dtype):
        if direct:
            return [jax.ShapeDtypeStruct(shape, dtype)] * count
        return [jax.ShapeDtypeStruct((count,) + shape, dtype)]

    taps = jnp.asarray(tap_matrix(half, TERMS))
    halo_shape = jax.ShapeDtypeStruct((HALO, columns), intensity.dtype)
    load_shapes = piece_shapes((SPREAD, rows, voxels), jnp.bfloat16)
    near_rows, far_rows, table, taps, alive, *loads = pl.pallas_call(
        lambda *refs: load_kernel(direct, count, slots, *refs),
        out_shape=[halo_shape, halo_shape]
        + [jax.ShapeDtypeStruct(x.shape, x.dtype) for x in (table, taps)]
        + [jax.ShapeDtypeStruct((8, offsets.shape[1]), jnp.float32)]
        + load_shapes,
        in_specs=[HBM] * 6,
        out_specs=[VMEM] * (5 + len(load_shapes)),
        scratch_shapes=[
            pltpu.SMEM(offsets.shape, jnp.int32),
            pltpu.SMEM(tile_count.shape, jnp.int32),
            pltpu.VMEM(volume.shape, volume.dtype),
            pltpu.SemaphoreType.DMA((8 + slots,)),
        ],
        compiler_params=params(16),
        name="loads",
    )(*[pltpu.with_memory_space_constraint(x, pltpu.HBM) for x in (offsets, tile_count, volume, table, taps, intensity[0])])
    near_rows, far_rows = swap_halos(near_rows, far_rows)
    arrived = exchange(direct, count, loads)

    tall = rows + 2 * HALO
    phase_map, inverse, sums, starts = pl.pallas_call(
        lambda *refs: phase_kernel(slots, *refs),
        out_shape=[
            jax.ShapeDtypeStruct((blocks, rows, half), jnp.float32),
            jax.ShapeDtypeStruct((padded_blocks, half), jnp.float32),
            jax.ShapeDtypeStruct((EXTRA_ROWS, half), jnp.float32),
            jax.ShapeDtypeStruct((-(-count // 8) * 8, half), jnp.int32),
        ],
        in_specs=[VMEM] * 7,
        out_specs=[VMEM] * 4,
        scratch_shapes=[
            pltpu.VMEM((tall, columns + 2 * half), intensity.dtype),
            pltpu.VMEM((blocks, tall, half), jnp.float32),
        ],
        compiler_params=params(16),
        name="phase",
    )(alive, offsets, intensity[0], near_rows, far_rows, table, taps)

    piece_shape = (2 * SPREAD * rows + EXTRA_ROWS, half)
    one_piece = jax.ShapeDtypeStruct(piece_shape, jnp.int16)
    first = list(range(count - 1, 0, -1))[:FIRST] if direct else []
    rest = [k for k in range(count) if k not in first]
    sent_shapes = [one_piece] * len(first) if direct else piece_shapes(piece_shape, jnp.int16)
    residual, windows, *sent = pl.pallas_call(
        lambda *refs: angle_kernel(direct, count, first, *refs),
        out_shape=[
            jax.ShapeDtypeStruct((blocks, rows, half), jnp.float32),
            jax.ShapeDtypeStruct((count, rows, (SPREAD + 1) * half), jnp.bfloat16),
        ]
        + sent_shapes,
        in_specs=[VMEM] * (5 + len(arrived)),
        out_specs=[VMEM] * (2 + len(sent_shapes)),
        scratch_shapes=[
            pltpu.VMEM((len(arrived), SPREAD * rows, voxels), jnp.float32),
        ],
        input_output_aliases={1: 0},
        compiler_params=params(16),
        name="angle",
    )(starts, phase_map, table, inverse, sums, *arrived)
    if direct:
        others = pl.pallas_call(
            lambda *refs: back_kernel(rest, *refs),
            out_shape=[one_piece] * len(rest),
            in_specs=[VMEM] * 3,
            out_specs=[VMEM] * len(rest),
            compiler_params=params(16),
            name="back",
        )(windows, table, sums)
        by_partner = dict(zip(first + rest, [*sent, *others]))
        sent = [by_partner[k] for k in range(count)]
    received = exchange(direct, count, sent)

    residual, plan = pl.pallas_call(
        lambda *refs: write_kernel(count, slots, *refs),
        out_shape=[
            jax.ShapeDtypeStruct((rows, columns), jnp.float32),
            jax.ShapeDtypeStruct((count + 8, half), jnp.int32),
        ],
        in_specs=[SMEM, SMEM, VMEM],
        out_specs=[VMEM, VMEM],
        compiler_params=params(16),
        name="write",
    )(offsets, tile_count, residual)

    def gather(ks, pieces, last, *earlier):
        flat = (slots, 2 * rows, half)
        shape = (slots, rows, voxels) if direct and last else flat
        return pl.pallas_call(
            lambda *refs: gather_kernel(direct, count, ks, slots, rows, last, *refs),
            out_shape=[
                jax.ShapeDtypeStruct(shape, jnp.float32),
                jax.ShapeDtypeStruct((8, half), jnp.float32),
            ],
            in_specs=[VMEM] * (1 + len(pieces) + len(earlier)),
            out_specs=[VMEM, VMEM],
            scratch_shapes=[
                pltpu.VMEM((len(pieces), 2 * SPREAD * rows, half), jnp.float32),
            ],
            compiler_params=params(16),
            name="gather_last" if last else "gather_first",
        )(plan, *pieces, *earlier)

    if direct:
        near = list(range(count // 2))
        far = list(range(count // 2, count))
        partial = gather(near, received[: count // 2], False)
        correction = gather(far, received[count // 2 :], True, *partial)[0]
    else:
        flat = gather(list(range(count)), received, True)[0]
        correction = jnp.swapaxes(flat.reshape(slots, 2, rows, half), 1, 2)
        correction = correction.reshape(slots, rows, voxels)
    return residual[None], correction


def solution(mesh):
    placed = (P("tile", "row", None), P("tile", "row", None), P("tile", None, None), P(), P())
    return jax.shard_map(
        local,
        mesh=mesh,
        in_specs=placed,
        out_specs=(P("tile", "row", None), P("tile", "row", None)),
        check_vma=False,
    )
```

```python
import jax
import jax.numpy as jnp
import numpy as np
from jax import lax
from jax.experimental import pallas as pl
from jax.experimental.pallas import tpu as pltpu
from jax.sharding import PartitionSpec as P


SPREAD = 4
RIM = 3
HALO = 8
GROUP = 22
TERMS = 2
FIRST = 1
HOME_ORDER = (7, 5, 6, 4, 3, 2, 1)
DIRECT_LIMIT = 16
EXTRA_ROWS = 8
SUM_SCALE = 2048.0
LOW_SCALE = 32000.0
CODE_TOP = 32000.0

decay_length = 2.0
row_floor = 0.5


SMEM = pl.BlockSpec(memory_space=pltpu.SMEM)
VMEM = pl.BlockSpec(memory_space=pltpu.VMEM)
HBM = pl.BlockSpec(memory_space=pltpu.HBM)


def params(mib):
    return pltpu.CompilerParams(vmem_limit_bytes=mib << 20)


def smoothing_taps():
    spread_taps = np.exp(-np.abs(np.arange(-RIM, RIM + 1)) / decay_length)
    return spread_taps / spread_taps.sum()


def each_piece(direct, count, member, refs, body):
    if direct:
        for k in range(count):
            body(refs[k], member ^ k)
    else:

        def step(k, carry):
            body(refs[0].at[k], k)
            return carry

        lax.fori_loop(0, count, step, 0)


def group_start(offsets, angle, group, slots):
    low = offsets[angle, group * slots]
    for j in range(1, slots):
        low = jnp.minimum(low, offsets[angle, group * slots + j])
    return low


def load_kernel(
    direct, count, slots, offsets_in, count_in, volume_in, table_in, taps_in, intensity, *refs
):
    lists = count if direct else 1
    near_rows, far_rows, table_out, taps_out, alive = refs[:5]
    pieces = refs[5 : 5 + lists]
    offsets, tile_count, volume, sems = refs[5 + lists :]
    member = lax.axis_index("tile")
    even = lax.rem(lax.axis_index("row"), 2) == 0
    last = intensity.shape[0] - HALO
    first_copy = pltpu.make_async_copy(offsets_in, offsets, sems.at[0])
    count_copy = pltpu.make_async_copy(count_in, tile_count, sems.at[1])
    near = pl.multiple_of(jnp.where(even, last, 0), HALO)
    far = pl.multiple_of(jnp.where(even, 0, last), HALO)
    near_copy = pltpu.make_async_copy(intensity.at[pl.ds(near, HALO)], near_rows, sems.at[3])
    far_copy = pltpu.make_async_copy(intensity.at[pl.ds(far, HALO)], far_rows, sems.at[4])
    later = [near_copy, far_copy]
    for i, (here, there) in enumerate(
        ((table_in, table_out), (taps_in, taps_out))
    ):
        later.append(pltpu.make_async_copy(here, there, sems.at[5 + i]))
    volume_copies = [
        pltpu.make_async_copy(volume_in.at[j], volume.at[j], sems.at[8 + j]) for j in range(slots)
    ]
    for copy in volume_copies:
        copy.start()
    first_copy.start()
    count_copy.start()
    for copy in later:
        copy.start()
    first_copy.wait()
    count_copy.wait()
    live = tile_count[member]
    for copy in volume_copies:
        copy.wait()

    def one(piece, angle):
        start = group_start(offsets, angle, member, slots)
        places = [offsets[angle, member * slots + j] - start for j in range(slots)]
        places = [jnp.where(j < live, places[j], -1) for j in range(slots)]
        for s in range(SPREAD):
            total = jnp.zeros(volume.shape[1:], jnp.float32)
            for j in range(slots):
                total = total + jnp.where(places[j] == s, 1.0, 0.0) * volume[j]
            piece[s] = total.astype(piece.dtype)

    each_piece(direct, count, member, pieces, one)
    lane = lax.broadcasted_iota(jnp.int32, alive.shape, 1)
    flags = jnp.zeros(alive.shape, jnp.float32)
    for g in range(alive.shape[1] // slots):
        here = (lane >= g * slots) & (lane < g * slots + tile_count[g])
        flags = jnp.where(here, 1.0, flags)
    alive[...] = flags
    for copy in later:
        copy.wait()


def tables(slots, blocks, offset_rows, alive, table, inverse, sums, starts):
    member = lax.axis_index("tile")
    half = table.shape[1] // 2
    padded = inverse.shape[0]
    total = offset_rows.shape[1]
    by_column = jnp.sum(table.astype(jnp.float32), axis=0, keepdims=True)
    mine = offset_rows[pl.ds(member, 1), :]
    group = lax.broadcasted_iota(jnp.int32, (starts.shape[0], total), 0)
    lane = lax.broadcasted_iota(jnp.int32, (starts.shape[0], total), 1)
    own = (lane >= group * slots) & (lane < (group + 1) * slots)
    lowest = jnp.min(jnp.where(own, mine, 1 << 20), axis=1, keepdims=True)
    starts[...] = jnp.broadcast_to(lowest, starts.shape)
    alive = alive[0:1, :]
    block = lax.broadcasted_iota(jnp.int32, (padded, total), 0)
    hits = jnp.where(block == mine, alive, 0.0)
    counts = jnp.sum(hits, axis=1, keepdims=True)
    before = jnp.sum(jnp.where(block == mine + 1, alive, 0.0), axis=1, keepdims=True)
    rows = counts * by_column[:, :half] + before * by_column[:, half:]
    inside = lax.broadcasted_iota(jnp.int32, (padded, half), 0) < blocks
    inverse[...] = jnp.where(inside, 1.0 / jnp.maximum(rows, row_floor), 0.0)
    ones = jnp.ones((8, table.shape[1]), table.dtype)
    by_voxel = lax.dot_general(
        ones, table, (((1,), (1,)), ((), ())), preferred_element_type=jnp.float32
    )[0:1]
    scaled = by_voxel * SUM_SCALE
    whole = jnp.floor(scaled)
    low = jnp.floor((scaled - whole) * LOW_SCALE + 0.5)
    packed = jnp.concatenate(
        [whole[:, :half], whole[:, half:], low[:, :half], low[:, half:]], axis=0
    )
    sums[...] = jnp.concatenate([packed, jnp.zeros((4, half), jnp.float32)], axis=0)


def tap_matrix(half, terms):
    place = np.arange(4 * half)[:, None] - half
    apart = np.abs(place - np.arange(2 * half)[None, :])
    taps = smoothing_taps()
    rest = np.where(apart <= RIM, np.exp(-apart / decay_length) * taps[RIM], 0.0)
    parts = []
    for _ in range(terms):
        part = rest.astype(jnp.bfloat16)
        parts.append(part)
        rest = rest - part.astype(np.float64)
    return np.concatenate(parts, axis=0)


def phase_kernel(slots, alive, offset_rows, intensity, near_rows, far_rows, footprint, *refs):
    taps, phase, inverse, sums, starts, padded, across = refs
    rows, columns = intensity.shape
    half = footprint.shape[1] // 2
    blocks = columns // half
    even = lax.rem(lax.axis_index("row"), 2) == 0
    decay = float(np.exp(-1.0 / decay_length))
    centre = float(smoothing_taps()[RIM])
    tall = rows + 2 * HALO
    edge = jnp.zeros((tall, half), padded.dtype)
    padded[:, :half] = edge
    padded[:, half + columns :] = edge
    inner = slice(half, half + columns)
    padded[HALO : HALO + rows, inner] = intensity[...]
    near = near_rows[...].astype(jnp.float32)
    far = far_rows[...].astype(jnp.float32)
    padded[:HALO, inner] = jnp.where(even, far, near).astype(padded.dtype)
    padded[HALO + rows :, inner] = jnp.where(even, near, far).astype(padded.dtype)
    tables(slots, blocks, offset_rows, alive, footprint[...], inverse, sums, starts)
    terms = taps.shape[0] // (4 * half)
    pairs = blocks // 2
    group = max(d for d in range(1, min(GROUP, pairs) + 1) if pairs % d == 0)
    stride = rows // 8

    def step(g, carry):
        tiles = [
            padded[:, pl.ds(pl.multiple_of((g * group + i) * 2 * half, half), 4 * half)]
            for i in range(group)
        ]
        stacked = jnp.concatenate([jnp.concatenate(tiles, axis=0)] * terms, axis=1)
        filtered = jnp.dot(stacked, taps[...], preferred_element_type=jnp.float32)
        for i in range(group):
            for h in range(2):
                across[(g * group + i) * 2 + h] = filtered[
                    i * tall : (i + 1) * tall, h * half : (h + 1) * half
                ]
        for i in range(2 * group):
            block = g * 2 * group + i
            lines = [
                across[block, pl.ds(HALO - RIM + m, 8, stride=stride), :]
                for m in range(stride + 2 * RIM)
            ]
            for k in range(stride):
                mid = k + RIM
                total = lines[mid - RIM] + lines[mid + RIM]
                for m in range(RIM - 1, 0, -1):
                    total = total * decay + (lines[mid - m] + lines[mid + m])
                total = total * decay + lines[mid]
                phase[block, pl.ds(k, 8, stride=stride), :] = -jnp.log(total * centre)
        return carry

    lax.fori_loop(0, pairs // group, step, 0)


def write_kernel(count, slots, offsets, tile_count, residual, out, plan):
    member = lax.axis_index("tile")
    lane = lax.broadcasted_iota(jnp.int32, (1, plan.shape[1]), 1)

    def one(angle, carry):
        start = group_start(offsets, angle, member, slots)
        row = jnp.zeros((1, plan.shape[1]), jnp.int32)
        for j in range(slots):
            row = jnp.where(lane == j, offsets[angle, member * slots + j] - start, row)
        plan[pl.ds(angle, 1), :] = row
        return carry

    lax.fori_loop(0, count, one, 0)
    plan[count : count + 1, :] = (lane < tile_count[member]).astype(jnp.int32)
    blocks, _, half = residual.shape
    for block in range(blocks):
        out[:, block * half : (block + 1) * half] = residual[block]


def encode(window, table, sums, piece):
    rows = window.shape[0]
    half = table.shape[1] // 2
    stacked = jnp.concatenate(
        [window[:, s * half : (s + 2) * half] for s in range(SPREAD)], axis=0
    )
    back = lax.dot_general(
        stacked, table, (((1,), (1,)), ((), ())), preferred_element_type=jnp.float32
    )
    top = jnp.max(jnp.max(jnp.abs(back), axis=0, keepdims=True), axis=1, keepdims=True)
    power = jnp.floor(jnp.log2(CODE_TOP / jnp.maximum(top, 1e-30)))
    code = jnp.round(back * jnp.exp2(power)).astype(jnp.int32)
    for s in range(SPREAD):
        for h in range(2):
            base = (2 * s + h) * rows
            piece[base : base + rows, :] = code[
                s * rows : (s + 1) * rows, h * half : (h + 1) * half
            ].astype(piece.dtype)
    base = 2 * SPREAD * rows
    line = lax.broadcasted_iota(jnp.int32, (EXTRA_ROWS, half), 0)
    extra = jnp.where(line < 4, sums, jnp.broadcast_to(power, (EXTRA_ROWS, half)))
    piece[base : base + EXTRA_ROWS, :] = extra.astype(jnp.int32).astype(piece.dtype)


def angle_kernel(
    direct, count, first, starts, phase, footprint, inverse, sums, *refs
):
    lists = count if direct else 1
    arrived, residual, windows = refs[:lists], refs[lists], refs[lists + 1]
    sent, images = refs[lists + 2 : -1], refs[-1]
    member = lax.axis_index("tile")
    table = footprint[...]
    blocks, rows, half = phase.shape
    voxels = footprint.shape[0]

    def project(piece, image):
        image[...] = jnp.dot(
            piece[...].reshape(SPREAD * rows, voxels), table, preferred_element_type=jnp.float32
        )

    def subtract(image, group):
        start = starts[group, 0]
        for s in range(SPREAD + 1):
            part = None
            if s < SPREAD:
                part = image[s * rows : (s + 1) * rows, :half]
            if s > 0:
                far = image[(s - 1) * rows : s * rows, half:]
                part = far if part is None else part + far
            block = start + s
            if s == SPREAD:
                part = jnp.where(block < blocks, part, 0.0)
                block = jnp.minimum(block, blocks - 1)
            residual[block] = residual[block] - part

    if direct:
        for k in range(count):
            project(arrived[k], images.at[k])
        for k in range(count):
            subtract(images.at[k], member ^ k)
    else:

        def one(k, carry):
            project(arrived[0].at[k], images.at[0])
            subtract(images.at[0], k)
            return carry

        lax.fori_loop(0, count, one, 0)

    def weigh(window, group):
        start = starts[group, 0]
        for s in range(SPREAD + 1):
            block = jnp.minimum(start + s, blocks - 1)
            scale = inverse[pl.ds(start + s, 1), :]
            window[:, s * half : (s + 1) * half] = (residual[block] * scale).astype(window.dtype)

    if direct:
        for k in first:
            weigh(windows.at[k], member ^ k)
        for piece, k in zip(sent, first):
            encode(windows[k], table, sums[...], piece)
        for k in range(count):
            if k not in first:
                weigh(windows.at[k], member ^ k)
    else:

        def step(k, carry):
            weigh(windows.at[k], k)
            encode(windows[k], table, sums[...], sent[0].at[k])
            return carry

        lax.fori_loop(0, count, step, 0)


def back_kernel(ks, windows, footprint, sums, *sent):
    for piece, k in zip(sent, ks):
        encode(windows[k], footprint[...], sums[...], piece)


def gather_kernel(direct, count, ks, slots, rows, last, plan, *refs):
    lists = len(ks) if direct else 1
    received = refs[:lists]
    refs = refs[lists:]
    earlier = None
    if direct and last:
        earlier, earlier_sums, refs = refs[0], refs[1], refs[2:]
    correction, column_sums, decoded = refs
    member = lax.axis_index("tile")
    half = column_sums.shape[1]
    base = 2 * SPREAD * rows

    def unpack(piece, into):
        extra = piece[base : base + EXTRA_ROWS, :].astype(jnp.float32)
        into[...] = piece[0:base, :].astype(jnp.float32) * jnp.exp2(-extra[4:5])
        return (extra[0:2] + extra[2:4] * (1.0 / LOW_SCALE)) * (1.0 / SUM_SCALE)

    def block_of(into, angle, j):
        at = plan[angle, j] * (2 * rows)
        return into[pl.ds(pl.multiple_of(at, 2 * rows), 2 * rows), :]

    if direct:
        total = earlier_sums[0:2] if last else jnp.zeros((2, half), jnp.float32)
        angles = [member ^ k for k in ks]
        for i, piece in enumerate(received):
            total = total + unpack(piece, decoded.at[i])
    else:
        column_sums[...] = jnp.zeros_like(column_sums)
        correction[...] = jnp.zeros_like(correction)

        def step(k, carry):
            column_sums[0:2] += unpack(received[0].at[k], decoded.at[0])
            for j in range(slots):
                correction[j] += block_of(decoded.at[0], k, j)
            return carry

        lax.fori_loop(0, len(ks), step, 0)
        total = column_sums[0:2]

    if last:
        inverse = 1.0 / total
    else:
        column_sums[0:2] = total
    for j in range(slots):
        if direct:
            sum_here = earlier[j] if last else None
            for i, angle in enumerate(angles):
                part = block_of(decoded.at[i], angle, j)
                sum_here = part if sum_here is None else sum_here + part
        else:
            sum_here = correction[j]
        if not last:
            correction[j] = sum_here
        elif direct:
            weight = jnp.where(plan[count, j] > 0, 1.0, 0.0)
            for h in range(2):
                correction[j, :, h * half : (h + 1) * half] = sum_here[
                    h * rows : (h + 1) * rows
                ] * (inverse[h : h + 1] * weight)
        else:
            weight = jnp.where(plan[count, j] > 0, 1.0, 0.0)
            correction[j] = sum_here * weight * jnp.concatenate(
                [jnp.broadcast_to(inverse[h : h + 1], (rows, half)) for h in range(2)], axis=0
            )


def exchange(direct, count, pieces):
    if not direct:
        return [lax.all_to_all(pieces[0], "tile", split_axis=0, concat_axis=0, tiled=True)]
    arrived = [pieces[0]]
    for k in range(1, count):
        arrived.append(lax.ppermute(pieces[k], "tile", [(i, i ^ k) for i in range(count)]))
    return arrived


def partner_order(count, wanted):
    known = [k for k in wanted if 0 < k < count]
    return known + [k for k in range(count - 1, 0, -1) if k not in known]


def swap_halos(near_rows, far_rows):
    count = lax.axis_size("row")
    pairs = [(i, i + 1) for i in range(0, count - 1, 2)]
    between = [(i, i + 1) for i in range(1, count - 1, 2)]
    far_rows = lax.ppermute(far_rows, "row", between + [(b, a) for a, b in between])
    near_rows = lax.ppermute(near_rows, "row", pairs + [(b, a) for a, b in pairs])
    return near_rows, far_rows


def use_direct(count):
    return count <= DIRECT_LIMIT and count & (count - 1) == 0


def local(intensity, volume, footprint, foot_offset, tile_count):
    count = lax.axis_size("tile")
    direct = use_direct(count)
    slots, rows, voxels = volume.shape
    angles_here, _, window = footprint.shape
    assert angles_here == 1
    half = window // 2
    columns = intensity.shape[2]
    blocks = columns // half
    padded_blocks = -(-(blocks + SPREAD + 1) // 8) * 8
    offsets = jnp.transpose(foot_offset)
    table = footprint[0]

    def piece_shapes(shape, dtype):
        if direct:
            return [jax.ShapeDtypeStruct(shape, dtype)] * count
        return [jax.ShapeDtypeStruct((count,) + shape, dtype)]

    taps = jnp.asarray(tap_matrix(half, TERMS))
    halo_shape = jax.ShapeDtypeStruct((HALO, columns), intensity.dtype)
    load_shapes = piece_shapes((SPREAD, rows, voxels), jnp.bfloat16)
    near_rows, far_rows, table, taps, alive, *loads = pl.pallas_call(
        lambda *refs: load_kernel(direct, count, slots, *refs),
        out_shape=[halo_shape, halo_shape]
        + [jax.ShapeDtypeStruct(x.shape, x.dtype) for x in (table, taps)]
        + [jax.ShapeDtypeStruct((8, offsets.shape[1]), jnp.float32)]
        + load_shapes,
        in_specs=[HBM] * 6,
        out_specs=[VMEM] * (5 + len(load_shapes)),
        scratch_shapes=[
            pltpu.SMEM(offsets.shape, jnp.int32),
            pltpu.SMEM(tile_count.shape, jnp.int32),
            pltpu.VMEM(volume.shape, volume.dtype),
            pltpu.SemaphoreType.DMA((8 + slots,)),
        ],
        compiler_params=params(16),
        name="loads",
    )(*[pltpu.with_memory_space_constraint(x, pltpu.HBM) for x in (offsets, tile_count, volume, table, taps, intensity[0])])
    near_rows, far_rows = swap_halos(near_rows, far_rows)
    arrived = exchange(direct, count, loads)

    tall = rows + 2 * HALO
    phase_map, inverse, sums, starts = pl.pallas_call(
        lambda *refs: phase_kernel(slots, *refs),
        out_shape=[
            jax.ShapeDtypeStruct((blocks, rows, half), jnp.float32),
            jax.ShapeDtypeStruct((padded_blocks, half), jnp.float32),
            jax.ShapeDtypeStruct((EXTRA_ROWS, half), jnp.float32),
            jax.ShapeDtypeStruct((-(-count // 8) * 8, half), jnp.int32),
        ],
        in_specs=[VMEM] * 7,
        out_specs=[VMEM] * 4,
        scratch_shapes=[
            pltpu.VMEM((tall, columns + 2 * half), intensity.dtype),
            pltpu.VMEM((blocks, tall, half), jnp.float32),
        ],
        compiler_params=params(16),
        name="phase",
    )(alive, offsets, intensity[0], near_rows, far_rows, table, taps)

    piece_shape = (2 * SPREAD * rows + EXTRA_ROWS, half)
    one_piece = jax.ShapeDtypeStruct(piece_shape, jnp.int16)
    first = partner_order(count, HOME_ORDER)[:FIRST] if direct else []
    rest = [k for k in range(count) if k not in first]
    sent_shapes = [one_piece] * len(first) if direct else piece_shapes(piece_shape, jnp.int16)
    residual, windows, *sent = pl.pallas_call(
        lambda *refs: angle_kernel(direct, count, first, *refs),
        out_shape=[
            jax.ShapeDtypeStruct((blocks, rows, half), jnp.float32),
            jax.ShapeDtypeStruct((count, rows, (SPREAD + 1) * half), jnp.bfloat16),
        ]
        + sent_shapes,
        in_specs=[VMEM] * (5 + len(arrived)),
        out_specs=[VMEM] * (2 + len(sent_shapes)),
        scratch_shapes=[
            pltpu.VMEM((len(arrived), SPREAD * rows, voxels), jnp.float32),
        ],
        input_output_aliases={1: 0},
        compiler_params=params(16),
        name="angle",
    )(starts, phase_map, table, inverse, sums, *arrived)
    if direct:
        others = pl.pallas_call(
            lambda *refs: back_kernel(rest, *refs),
            out_shape=[one_piece] * len(rest),
            in_specs=[VMEM] * 3,
            out_specs=[VMEM] * len(rest),
            compiler_params=params(16),
            name="back",
        )(windows, table, sums)
        by_partner = dict(zip(first + rest, [*sent, *others]))
        sent = [by_partner[k] for k in range(count)]
    received = exchange(direct, count, sent)

    residual, plan = pl.pallas_call(
        lambda *refs: write_kernel(count, slots, *refs),
        out_shape=[
            jax.ShapeDtypeStruct((rows, columns), jnp.float32),
            jax.ShapeDtypeStruct((count + 8, half), jnp.int32),
        ],
        in_specs=[SMEM, SMEM, VMEM],
        out_specs=[VMEM, VMEM],
        compiler_params=params(16),
        name="write",
    )(offsets, tile_count, residual)

    def gather(ks, pieces, last, *earlier):
        flat = (slots, 2 * rows, half)
        shape = (slots, rows, voxels) if direct and last else flat
        return pl.pallas_call(
            lambda *refs: gather_kernel(direct, count, ks, slots, rows, last, *refs),
            out_shape=[
                jax.ShapeDtypeStruct(shape, jnp.float32),
                jax.ShapeDtypeStruct((8, half), jnp.float32),
            ],
            in_specs=[VMEM] * (1 + len(pieces) + len(earlier)),
            out_specs=[VMEM, VMEM],
            scratch_shapes=[
                pltpu.VMEM((len(pieces), 2 * SPREAD * rows, half), jnp.float32),
            ],
            compiler_params=params(16),
            name="gather_last" if last else "gather_first",
        )(plan, *pieces, *earlier)

    if direct:
        near = list(range(count // 2))
        far = list(range(count // 2, count))
        partial = gather(near, received[: count // 2], False)
        correction = gather(far, received[count // 2 :], True, *partial)[0]
    else:
        flat = gather(list(range(count)), received, True)[0]
        correction = jnp.swapaxes(flat.reshape(slots, 2, rows, half), 1, 2)
        correction = correction.reshape(slots, rows, voxels)
    return residual[None], correction


def solution(mesh):
    placed = (P("tile", "row", None), P("tile", "row", None), P("tile", None, None), P(), P())
    return jax.shard_map(
        local,
        mesh=mesh,
        in_specs=placed,
        out_specs=(P("tile", "row", None), P("tile", "row", None)),
        check_vma=False,
    )
```

```python
import jax
import jax.numpy as jnp
import numpy as np
from jax import lax
from jax.experimental import pallas as pl
from jax.experimental.pallas import tpu as pltpu
from jax.sharding import PartitionSpec as P


SPREAD = 4
RIM = 3
HALO = 8
GROUP = 22
TERMS = 2
FIRST = 1
LATE = 2
OUT_ORDER = (7, 5, 6, 4, 3, 2, 1)
HOME_ORDER = (6, 5, 7, 4, 3, 1, 2)
DIRECT_LIMIT = 16
EXTRA_ROWS = 8
SUM_SCALE = 2048.0
LOW_SCALE = 32000.0
CODE_TOP = 32000.0

decay_length = 2.0
row_floor = 0.5


SMEM = pl.BlockSpec(memory_space=pltpu.SMEM)
VMEM = pl.BlockSpec(memory_space=pltpu.VMEM)
HBM = pl.BlockSpec(memory_space=pltpu.HBM)


def params(mib):
    return pltpu.CompilerParams(vmem_limit_bytes=mib << 20)


def smoothing_taps():
    spread_taps = np.exp(-np.abs(np.arange(-RIM, RIM + 1)) / decay_length)
    return spread_taps / spread_taps.sum()


def each_piece(direct, count, member, refs, body):
    if direct:
        for k in range(count):
            body(refs[k], member ^ k)
    else:

        def step(k, carry):
            body(refs[0].at[k], k)
            return carry

        lax.fori_loop(0, count, step, 0)


def group_start(offsets, angle, group, slots):
    low = offsets[angle, group * slots]
    for j in range(1, slots):
        low = jnp.minimum(low, offsets[angle, group * slots + j])
    return low


def load_kernel(
    direct, count, slots, offsets_in, count_in, volume_in, table_in, intensity, *refs
):
    lists = count if direct else 1
    near_rows, far_rows, table_out, offsets_out, alive = refs[:5]
    pieces = refs[5 : 5 + lists]
    offsets, tile_count, volume, sems = refs[5 + lists :]
    member = lax.axis_index("tile")
    even = lax.rem(lax.axis_index("row"), 2) == 0
    last = intensity.shape[0] - HALO
    first_copy = pltpu.make_async_copy(offsets_in, offsets, sems.at[0])
    count_copy = pltpu.make_async_copy(count_in, tile_count, sems.at[1])
    near = pl.multiple_of(jnp.where(even, last, 0), HALO)
    far = pl.multiple_of(jnp.where(even, 0, last), HALO)
    near_copy = pltpu.make_async_copy(intensity.at[pl.ds(near, HALO)], near_rows, sems.at[3])
    far_copy = pltpu.make_async_copy(intensity.at[pl.ds(far, HALO)], far_rows, sems.at[4])
    table_copy = pltpu.make_async_copy(table_in, table_out, sems.at[5])
    rows_copy = pltpu.make_async_copy(offsets_in, offsets_out, sems.at[6])
    later = [near_copy, far_copy, table_copy, rows_copy]
    volume_copies = [
        pltpu.make_async_copy(volume_in.at[j], volume.at[j], sems.at[7 + j]) for j in range(slots)
    ]
    for copy in volume_copies:
        copy.start()
    first_copy.start()
    count_copy.start()
    for copy in later:
        copy.start()
    first_copy.wait()
    count_copy.wait()
    live = tile_count[member]
    for copy in volume_copies:
        copy.wait()

    def one(piece, angle):
        start = group_start(offsets, angle, member, slots)
        places = [offsets[angle, member * slots + j] - start for j in range(slots)]
        places = [jnp.where(j < live, places[j], -1) for j in range(slots)]
        for s in range(SPREAD):
            total = jnp.zeros(volume.shape[1:], jnp.float32)
            for j in range(slots):
                total = total + jnp.where(places[j] == s, 1.0, 0.0) * volume[j]
            piece[s] = total.astype(piece.dtype)

    each_piece(direct, count, member, pieces, one)
    lane = lax.broadcasted_iota(jnp.int32, alive.shape, 1)
    flags = jnp.zeros(alive.shape, jnp.float32)
    for g in range(alive.shape[1] // slots):
        here = (lane >= g * slots) & (lane < g * slots + tile_count[g])
        flags = jnp.where(here, 1.0, flags)
    alive[...] = flags
    for copy in later:
        copy.wait()


def tables(slots, blocks, offset_rows, alive, table, inverse, sums, starts):
    member = lax.axis_index("tile")
    half = table.shape[1] // 2
    padded = inverse.shape[0]
    total = offset_rows.shape[1]
    by_column = jnp.sum(table.astype(jnp.float32), axis=0, keepdims=True)
    mine = offset_rows[pl.ds(member, 1), :]
    group = lax.broadcasted_iota(jnp.int32, (starts.shape[0], total), 0)
    lane = lax.broadcasted_iota(jnp.int32, (starts.shape[0], total), 1)
    own = (lane >= group * slots) & (lane < (group + 1) * slots)
    lowest = jnp.min(jnp.where(own, mine, 1 << 20), axis=1, keepdims=True)
    starts[...] = jnp.broadcast_to(lowest, starts.shape)
    alive = alive[0:1, :]
    block = lax.broadcasted_iota(jnp.int32, (padded, total), 0)
    hits = jnp.where(block == mine, alive, 0.0)
    counts = jnp.sum(hits, axis=1, keepdims=True)
    before = jnp.sum(jnp.where(block == mine + 1, alive, 0.0), axis=1, keepdims=True)
    rows = counts * by_column[:, :half] + before * by_column[:, half:]
    inside = lax.broadcasted_iota(jnp.int32, (padded, half), 0) < blocks
    inverse[...] = jnp.where(inside, 1.0 / jnp.maximum(rows, row_floor), 0.0)
    ones = jnp.ones((8, table.shape[1]), table.dtype)
    by_voxel = lax.dot_general(
        ones, table, (((1,), (1,)), ((), ())), preferred_element_type=jnp.float32
    )[0:1]
    scaled = by_voxel * SUM_SCALE
    whole = jnp.floor(scaled)
    low = jnp.floor((scaled - whole) * LOW_SCALE + 0.5)
    packed = jnp.concatenate(
        [whole[:, :half], whole[:, half:], low[:, :half], low[:, half:]], axis=0
    )
    sums[...] = jnp.concatenate([packed, jnp.zeros((4, half), jnp.float32)], axis=0)


def tap_terms(terms):
    rest = smoothing_taps()[RIM:]
    parts = []
    for _ in range(terms):
        part = rest.astype(jnp.bfloat16).astype(np.float64)
        parts.append([float(v) for v in part])
        rest = rest - part
    return parts


def build_taps(taps, half, terms):
    row = lax.broadcasted_iota(jnp.int32, (half, half), 0)
    column = lax.broadcasted_iota(jnp.int32, (half, half), 1)
    parts = tap_terms(terms)
    for shift in (-1, 0, 1):
        apart = jnp.abs(row - column + shift * half)
        for term in range(terms):
            value = jnp.zeros((half, half), jnp.float32)
            for distance in range(RIM + 1):
                value = jnp.where(apart == distance, parts[term][distance], value)
            value = value.astype(taps.dtype)
            for side in range(2):
                base = (4 * term + 1 + side + shift) * half
                taps[base : base + half, side * half : (side + 1) * half] = value
    nothing = jnp.zeros((half, half), taps.dtype)
    for term in range(terms):
        taps[4 * term * half : (4 * term + 1) * half, half:] = nothing
        taps[(4 * term + 3) * half : (4 * term + 4) * half, :half] = nothing


def phase_kernel(slots, alive, offset_rows, intensity, near_rows, far_rows, footprint, *refs):
    phase, inverse, sums, starts, padded, across, taps = refs
    rows, columns = intensity.shape
    half = footprint.shape[1] // 2
    blocks = columns // half
    even = lax.rem(lax.axis_index("row"), 2) == 0
    decay = float(np.exp(-1.0 / decay_length))
    centre = float(smoothing_taps()[RIM])
    tall = rows + 2 * HALO
    edge = jnp.zeros((tall, half), padded.dtype)
    padded[:, :half] = edge
    padded[:, half + columns :] = edge
    inner = slice(half, half + columns)
    padded[HALO : HALO + rows, inner] = intensity[...]
    near = near_rows[...].astype(jnp.float32)
    far = far_rows[...].astype(jnp.float32)
    padded[:HALO, inner] = jnp.where(even, far, near).astype(padded.dtype)
    padded[HALO + rows :, inner] = jnp.where(even, near, far).astype(padded.dtype)
    build_taps(taps, half, TERMS)
    tables(slots, blocks, offset_rows, alive, footprint[...], inverse, sums, starts)
    terms = TERMS
    pairs = blocks // 2
    group = max(d for d in range(1, min(GROUP, pairs) + 1) if pairs % d == 0)
    stride = rows // 8

    def step(g, carry):
        tiles = [
            padded[:, pl.ds(pl.multiple_of((g * group + i) * 2 * half, half), 4 * half)]
            for i in range(group)
        ]
        stacked = jnp.concatenate([jnp.concatenate(tiles, axis=0)] * terms, axis=1)
        filtered = jnp.dot(stacked, taps[...], preferred_element_type=jnp.float32)
        for i in range(group):
            for h in range(2):
                across[(g * group + i) * 2 + h] = filtered[
                    i * tall : (i + 1) * tall, h * half : (h + 1) * half
                ]
        for i in range(2 * group):
            block = g * 2 * group + i
            lines = [
                across[block, pl.ds(HALO - RIM + m, 8, stride=stride), :]
                for m in range(stride + 2 * RIM)
            ]
            for k in range(stride):
                mid = k + RIM
                total = lines[mid - RIM] + lines[mid + RIM]
                for m in range(RIM - 1, 0, -1):
                    total = total * decay + (lines[mid - m] + lines[mid + m])
                total = total * decay + lines[mid]
                phase[block, pl.ds(k, 8, stride=stride), :] = -jnp.log(total * centre)
        return carry

    lax.fori_loop(0, pairs // group, step, 0)


def write_kernel(count, slots, offsets, tile_count, residual, out, plan):
    member = lax.axis_index("tile")
    lane = lax.broadcasted_iota(jnp.int32, (1, plan.shape[1]), 1)

    def one(angle, carry):
        start = group_start(offsets, angle, member, slots)
        row = jnp.zeros((1, plan.shape[1]), jnp.int32)
        for j in range(slots):
            row = jnp.where(lane == j, offsets[angle, member * slots + j] - start, row)
        plan[pl.ds(angle, 1), :] = row
        return carry

    lax.fori_loop(0, count, one, 0)
    plan[count : count + 1, :] = (lane < tile_count[member]).astype(jnp.int32)
    blocks, _, half = residual.shape
    for block in range(blocks):
        out[:, block * half : (block + 1) * half] = residual[block]


def encode(window, table, sums, piece):
    rows = window.shape[0]
    half = table.shape[1] // 2
    stacked = jnp.concatenate(
        [window[:, s * half : (s + 2) * half] for s in range(SPREAD)], axis=0
    )
    back = lax.dot_general(
        stacked, table, (((1,), (1,)), ((), ())), preferred_element_type=jnp.float32
    )
    top = jnp.max(jnp.max(jnp.abs(back), axis=0, keepdims=True), axis=1, keepdims=True)
    power = jnp.floor(jnp.log2(CODE_TOP / jnp.maximum(top, 1e-30)))
    code = jnp.round(back * jnp.exp2(power)).astype(jnp.int32)
    for s in range(SPREAD):
        for h in range(2):
            base = (2 * s + h) * rows
            piece[base : base + rows, :] = code[
                s * rows : (s + 1) * rows, h * half : (h + 1) * half
            ].astype(piece.dtype)
    base = 2 * SPREAD * rows
    line = lax.broadcasted_iota(jnp.int32, (EXTRA_ROWS, half), 0)
    extra = jnp.where(line < 4, sums, jnp.broadcast_to(power, (EXTRA_ROWS, half)))
    piece[base : base + EXTRA_ROWS, :] = extra.astype(jnp.int32).astype(piece.dtype)


def subtract_loads(ks, starts, arrived, table, residual, images):
    member = lax.axis_index("tile")
    blocks, rows, half = residual.shape

    def project(piece, image):
        image[...] = jnp.dot(
            piece[...].reshape(SPREAD * rows, table.shape[0]),
            table,
            preferred_element_type=jnp.float32,
        )

    def subtract(image, group):
        start = starts[group, 0]
        for s in range(SPREAD + 1):
            part = None
            if s < SPREAD:
                part = image[s * rows : (s + 1) * rows, :half]
            if s > 0:
                far = image[(s - 1) * rows : s * rows, half:]
                part = far if part is None else part + far
            block = start + s
            if s == SPREAD:
                part = jnp.where(block < blocks, part, 0.0)
                block = jnp.minimum(block, blocks - 1)
            residual[block] = residual[block] - part

    if len(arrived) == len(ks):
        for i, piece in enumerate(arrived):
            project(piece, images.at[i])
        for i, k in enumerate(ks):
            subtract(images.at[i], member ^ k)
    else:

        def one(k, carry):
            project(arrived[0].at[k], images.at[0])
            subtract(images.at[0], k)
            return carry

        lax.fori_loop(0, len(ks), one, 0)


def early_kernel(ks, starts, phase, footprint, *refs):
    arrived, residual, images = refs[: len(ks)], refs[-2], refs[-1]
    subtract_loads(ks, starts, arrived, footprint[...], residual, images)


def angle_kernel(direct, count, ks, first, starts, phase, footprint, inverse, sums, *refs):
    lists = len(ks) if direct else 1
    arrived, residual, windows = refs[:lists], refs[lists], refs[lists + 1]
    sent, images = refs[lists + 2 : -1], refs[-1]
    member = lax.axis_index("tile")
    table = footprint[...]
    blocks, _, half = phase.shape
    subtract_loads(ks, starts, arrived, table, residual, images)

    def weigh(window, group):
        start = starts[group, 0]
        for s in range(SPREAD + 1):
            block = jnp.minimum(start + s, blocks - 1)
            scale = inverse[pl.ds(start + s, 1), :]
            window[:, s * half : (s + 1) * half] = (residual[block] * scale).astype(window.dtype)

    if direct:
        for k in first:
            weigh(windows.at[k], member ^ k)
        for piece, k in zip(sent, first):
            encode(windows[k], table, sums[...], piece)
        for k in range(count):
            if k not in first:
                weigh(windows.at[k], member ^ k)
    else:

        def step(k, carry):
            weigh(windows.at[k], k)
            encode(windows[k], table, sums[...], sent[0].at[k])
            return carry

        lax.fori_loop(0, count, step, 0)


def back_kernel(ks, windows, footprint, sums, *sent):
    for piece, k in zip(sent, ks):
        encode(windows[k], footprint[...], sums[...], piece)


def gather_kernel(direct, count, ks, slots, rows, last, plan, *refs):
    lists = len(ks) if direct else 1
    received = refs[:lists]
    refs = refs[lists:]
    earlier = None
    if direct and last:
        earlier, earlier_sums, refs = refs[0], refs[1], refs[2:]
    correction, column_sums, decoded = refs
    member = lax.axis_index("tile")
    half = column_sums.shape[1]
    base = 2 * SPREAD * rows

    def unpack(piece, into):
        extra = piece[base : base + EXTRA_ROWS, :].astype(jnp.float32)
        into[...] = piece[0:base, :].astype(jnp.float32) * jnp.exp2(-extra[4:5])
        return (extra[0:2] + extra[2:4] * (1.0 / LOW_SCALE)) * (1.0 / SUM_SCALE)

    def block_of(into, angle, j):
        at = plan[angle, j] * (2 * rows)
        return into[pl.ds(pl.multiple_of(at, 2 * rows), 2 * rows), :]

    if direct:
        total = earlier_sums[0:2] if last else jnp.zeros((2, half), jnp.float32)
        angles = [member ^ k for k in ks]
        for i, piece in enumerate(received):
            total = total + unpack(piece, decoded.at[i])
    else:
        column_sums[...] = jnp.zeros_like(column_sums)
        correction[...] = jnp.zeros_like(correction)

        def step(k, carry):
            column_sums[0:2] += unpack(received[0].at[k], decoded.at[0])
            for j in range(slots):
                correction[j] += block_of(decoded.at[0], k, j)
            return carry

        lax.fori_loop(0, len(ks), step, 0)
        total = column_sums[0:2]

    if last:
        inverse = 1.0 / total
    else:
        column_sums[0:2] = total
    for j in range(slots):
        if direct:
            sum_here = earlier[j] if last else None
            for i, angle in enumerate(angles):
                part = block_of(decoded.at[i], angle, j)
                sum_here = part if sum_here is None else sum_here + part
        else:
            sum_here = correction[j]
        if not last:
            correction[j] = sum_here
        elif direct:
            weight = jnp.where(plan[count, j] > 0, 1.0, 0.0)
            for h in range(2):
                correction[j, :, h * half : (h + 1) * half] = sum_here[
                    h * rows : (h + 1) * rows
                ] * (inverse[h : h + 1] * weight)
        else:
            weight = jnp.where(plan[count, j] > 0, 1.0, 0.0)
            correction[j] = sum_here * weight * jnp.concatenate(
                [jnp.broadcast_to(inverse[h : h + 1], (rows, half)) for h in range(2)], axis=0
            )


def exchange(direct, count, pieces):
    if not direct:
        return [lax.all_to_all(pieces[0], "tile", split_axis=0, concat_axis=0, tiled=True)]
    arrived = [pieces[0]]
    for k in range(1, count):
        arrived.append(lax.ppermute(pieces[k], "tile", [(i, i ^ k) for i in range(count)]))
    return arrived


def partner_order(count, wanted):
    known = [k for k in wanted if 0 < k < count]
    return known + [k for k in range(count - 1, 0, -1) if k not in known]


def swap_halos(near_rows, far_rows):
    count = lax.axis_size("row")
    pairs = [(i, i + 1) for i in range(0, count - 1, 2)]
    between = [(i, i + 1) for i in range(1, count - 1, 2)]
    far_rows = lax.ppermute(far_rows, "row", between + [(b, a) for a, b in between])
    near_rows = lax.ppermute(near_rows, "row", pairs + [(b, a) for a, b in pairs])
    return near_rows, far_rows


def use_direct(count):
    return count <= DIRECT_LIMIT and count & (count - 1) == 0


def local(intensity, volume, footprint, foot_offset, tile_count):
    count = lax.axis_size("tile")
    direct = use_direct(count)
    slots, rows, voxels = volume.shape
    angles_here, _, window = footprint.shape
    assert angles_here == 1
    half = window // 2
    columns = intensity.shape[2]
    blocks = columns // half
    padded_blocks = -(-(blocks + SPREAD + 1) // 8) * 8
    offsets = jnp.transpose(foot_offset)
    table = footprint[0]

    def piece_shapes(shape, dtype):
        if direct:
            return [jax.ShapeDtypeStruct(shape, dtype)] * count
        return [jax.ShapeDtypeStruct((count,) + shape, dtype)]

    halo_shape = jax.ShapeDtypeStruct((HALO, columns), intensity.dtype)
    load_shapes = piece_shapes((SPREAD, rows, voxels), jnp.bfloat16)
    near_rows, far_rows, table, offset_rows, alive, *loads = pl.pallas_call(
        lambda *refs: load_kernel(direct, count, slots, *refs),
        out_shape=[halo_shape, halo_shape]
        + [jax.ShapeDtypeStruct(x.shape, x.dtype) for x in (table, offsets)]
        + [jax.ShapeDtypeStruct((8, offsets.shape[1]), jnp.float32)]
        + load_shapes,
        in_specs=[HBM] * 5,
        out_specs=[VMEM] * (5 + len(load_shapes)),
        scratch_shapes=[
            pltpu.SMEM(offsets.shape, jnp.int32),
            pltpu.SMEM(tile_count.shape, jnp.int32),
            pltpu.VMEM(volume.shape, volume.dtype),
            pltpu.SemaphoreType.DMA((7 + slots,)),
        ],
        compiler_params=params(16),
        name="loads",
    )(*[pltpu.with_memory_space_constraint(x, pltpu.HBM) for x in (offsets, tile_count, volume, table, intensity[0])])
    near_rows, far_rows = swap_halos(near_rows, far_rows)
    arrived = exchange(direct, count, loads)

    tall = rows + 2 * HALO
    phase_map, inverse, sums, starts = pl.pallas_call(
        lambda *refs: phase_kernel(slots, *refs),
        out_shape=[
            jax.ShapeDtypeStruct((blocks, rows, half), jnp.float32),
            jax.ShapeDtypeStruct((padded_blocks, half), jnp.float32),
            jax.ShapeDtypeStruct((EXTRA_ROWS, half), jnp.float32),
            jax.ShapeDtypeStruct((-(-count // 8) * 8, half), jnp.int32),
        ],
        in_specs=[VMEM] * 6,
        out_specs=[VMEM] * 4,
        scratch_shapes=[
            pltpu.VMEM((tall, columns + 2 * half), intensity.dtype),
            pltpu.VMEM((blocks, tall, half), jnp.float32),
            pltpu.VMEM((4 * TERMS * half, 2 * half), jnp.bfloat16),
        ],
        compiler_params=params(16),
        name="phase",
    )(alive, offset_rows, intensity[0], near_rows, far_rows, table)

    piece_shape = (2 * SPREAD * rows + EXTRA_ROWS, half)
    one_piece = jax.ShapeDtypeStruct(piece_shape, jnp.int16)
    first = partner_order(count, HOME_ORDER)[:FIRST] if direct else []
    rest = [k for k in range(count) if k not in first]
    sent_shapes = [one_piece] * len(first) if direct else piece_shapes(piece_shape, jnp.int16)
    grid_shape = jax.ShapeDtypeStruct((blocks, rows, half), jnp.float32)
    late = partner_order(count, OUT_ORDER)[-LATE:] if direct else list(range(count))
    if direct:
        early = [k for k in range(count) if k not in late]
        phase_map = pl.pallas_call(
            lambda *refs: early_kernel(early, *refs),
            out_shape=grid_shape,
            in_specs=[VMEM] * (3 + len(early)),
            out_specs=VMEM,
            scratch_shapes=[pltpu.VMEM((len(early), SPREAD * rows, voxels), jnp.float32)],
            input_output_aliases={1: 0},
            compiler_params=params(16),
            name="early",
        )(starts, phase_map, table, *[arrived[k] for k in early])
        arrived = [arrived[k] for k in late]
    residual, windows, *sent = pl.pallas_call(
        lambda *refs: angle_kernel(direct, count, late, first, *refs),
        out_shape=[
            grid_shape,
            jax.ShapeDtypeStruct((count, rows, (SPREAD + 1) * half), jnp.bfloat16),
        ]
        + sent_shapes,
        in_specs=[VMEM] * (5 + len(arrived)),
        out_specs=[VMEM] * (2 + len(sent_shapes)),
        scratch_shapes=[
            pltpu.VMEM((len(arrived), SPREAD * rows, voxels), jnp.float32),
        ],
        input_output_aliases={1: 0},
        compiler_params=params(16),
        name="angle",
    )(starts, phase_map, table, inverse, sums, *arrived)
    if direct:
        others = pl.pallas_call(
            lambda *refs: back_kernel(rest, *refs),
            out_shape=[one_piece] * len(rest),
            in_specs=[VMEM] * 3,
            out_specs=[VMEM] * len(rest),
            compiler_params=params(16),
            name="back",
        )(windows, table, sums)
        by_partner = dict(zip(first + rest, [*sent, *others]))
        sent = [by_partner[k] for k in range(count)]
    received = exchange(direct, count, sent)

    residual, plan = pl.pallas_call(
        lambda *refs: write_kernel(count, slots, *refs),
        out_shape=[
            jax.ShapeDtypeStruct((rows, columns), jnp.float32),
            jax.ShapeDtypeStruct((count + 8, half), jnp.int32),
        ],
        in_specs=[SMEM, SMEM, VMEM],
        out_specs=[VMEM, VMEM],
        compiler_params=params(16),
        name="write",
    )(offset_rows, tile_count, residual)

    def gather(ks, pieces, last, *earlier):
        flat = (slots, 2 * rows, half)
        shape = (slots, rows, voxels) if direct and last else flat
        return pl.pallas_call(
            lambda *refs: gather_kernel(direct, count, ks, slots, rows, last, *refs),
            out_shape=[
                jax.ShapeDtypeStruct(shape, jnp.float32),
                jax.ShapeDtypeStruct((8, half), jnp.float32),
            ],
            in_specs=[VMEM] * (1 + len(pieces) + len(earlier)),
            out_specs=[VMEM, VMEM],
            scratch_shapes=[
                pltpu.VMEM((len(pieces), 2 * SPREAD * rows, half), jnp.float32),
            ],
            compiler_params=params(16),
            name="gather_last" if last else "gather_first",
        )(plan, *pieces, *earlier)

    if direct:
        last = [0] + partner_order(count, HOME_ORDER)[-LATE:]
        soon = [k for k in range(count) if k not in last]
        partial = gather(soon, [received[k] for k in soon], False)
        correction = gather(last, [received[k] for k in last], True, *partial)[0]
    else:
        flat = gather(list(range(count)), received, True)[0]
        correction = jnp.swapaxes(flat.reshape(slots, 2, rows, half), 1, 2)
        correction = correction.reshape(slots, rows, voxels)
    return residual[None], correction


def solution(mesh):
    placed = (P("tile", "row", None), P("tile", "row", None), P("tile", None, None), P(), P())
    return jax.shard_map(
        local,
        mesh=mesh,
        in_specs=placed,
        out_specs=(P("tile", "row", None), P("tile", "row", None)),
        check_vma=False,
    )
```

```python
import jax
import jax.numpy as jnp
import numpy as np
from jax import lax
from jax.experimental import pallas as pl
from jax.experimental.pallas import tpu as pltpu
from jax.sharding import PartitionSpec as P


SPREAD = 4
RIM = 3
HALO = 8
GROUP = 22
TERMS = 2
FIRST = 2
LATE = 3
OUT_ORDER = (7, 5, 6, 4, 3, 2, 1)
HOME_ORDER = (6, 5, 7, 4, 3, 2, 1)
DIRECT_LIMIT = 16
EXTRA_ROWS = 8
SUM_SCALE = 2048.0
LOW_SCALE = 32000.0
CODE_TOP = 32000.0

decay_length = 2.0
row_floor = 0.5


SMEM = pl.BlockSpec(memory_space=pltpu.SMEM)
VMEM = pl.BlockSpec(memory_space=pltpu.VMEM)
HBM = pl.BlockSpec(memory_space=pltpu.HBM)


def params(mib):
    return pltpu.CompilerParams(vmem_limit_bytes=mib << 20)


def smoothing_taps():
    spread_taps = np.exp(-np.abs(np.arange(-RIM, RIM + 1)) / decay_length)
    return spread_taps / spread_taps.sum()


def each_piece(direct, count, member, refs, body):
    if direct:
        for k in range(count):
            body(refs[k], member ^ k)
    else:

        def step(k, carry):
            body(refs[0].at[k], k)
            return carry

        lax.fori_loop(0, count, step, 0)


def group_start(offsets, angle, group, slots):
    low = offsets[angle, group * slots]
    for j in range(1, slots):
        low = jnp.minimum(low, offsets[angle, group * slots + j])
    return low


def load_kernel(
    direct, count, slots, offsets_in, count_in, volume_in, table_in, intensity, *refs
):
    lists = count if direct else 1
    near_rows, far_rows, table_out, offsets_out, alive = refs[:5]
    pieces = refs[5 : 5 + lists]
    offsets, tile_count, volume, sems = refs[5 + lists :]
    member = lax.axis_index("tile")
    even = lax.rem(lax.axis_index("row"), 2) == 0
    last = intensity.shape[0] - HALO
    first_copy = pltpu.make_async_copy(offsets_in, offsets, sems.at[0])
    count_copy = pltpu.make_async_copy(count_in, tile_count, sems.at[1])
    near = pl.multiple_of(jnp.where(even, last, 0), HALO)
    far = pl.multiple_of(jnp.where(even, 0, last), HALO)
    near_copy = pltpu.make_async_copy(intensity.at[pl.ds(near, HALO)], near_rows, sems.at[3])
    far_copy = pltpu.make_async_copy(intensity.at[pl.ds(far, HALO)], far_rows, sems.at[4])
    table_copy = pltpu.make_async_copy(table_in, table_out, sems.at[5])
    rows_copy = pltpu.make_async_copy(offsets_in, offsets_out, sems.at[6])
    later = [near_copy, far_copy, table_copy, rows_copy]
    volume_copies = [
        pltpu.make_async_copy(volume_in.at[j], volume.at[j], sems.at[7 + j]) for j in range(slots)
    ]
    for copy in volume_copies:
        copy.start()
    first_copy.start()
    count_copy.start()
    for copy in later:
        copy.start()
    first_copy.wait()
    count_copy.wait()
    live = tile_count[member]
    for copy in volume_copies:
        copy.wait()

    def one(piece, angle):
        start = group_start(offsets, angle, member, slots)
        places = [offsets[angle, member * slots + j] - start for j in range(slots)]
        places = [jnp.where(j < live, places[j], -1) for j in range(slots)]
        for s in range(SPREAD):
            total = jnp.zeros(volume.shape[1:], jnp.float32)
            for j in range(slots):
                total = total + jnp.where(places[j] == s, 1.0, 0.0) * volume[j]
            piece[s] = total.astype(piece.dtype)

    each_piece(direct, count, member, pieces, one)
    lane = lax.broadcasted_iota(jnp.int32, alive.shape, 1)
    flags = jnp.zeros(alive.shape, jnp.float32)
    for g in range(alive.shape[1] // slots):
        here = (lane >= g * slots) & (lane < g * slots + tile_count[g])
        flags = jnp.where(here, 1.0, flags)
    alive[...] = flags
    for copy in later:
        copy.wait()


def tables(slots, blocks, offset_rows, alive, table, inverse, sums, starts):
    member = lax.axis_index("tile")
    half = table.shape[1] // 2
    padded = inverse.shape[0]
    total = offset_rows.shape[1]
    by_column = jnp.sum(table.astype(jnp.float32), axis=0, keepdims=True)
    mine = offset_rows[pl.ds(member, 1), :]
    group = lax.broadcasted_iota(jnp.int32, (starts.shape[0], total), 0)
    lane = lax.broadcasted_iota(jnp.int32, (starts.shape[0], total), 1)
    own = (lane >= group * slots) & (lane < (group + 1) * slots)
    lowest = jnp.min(jnp.where(own, mine, 1 << 20), axis=1, keepdims=True)
    starts[...] = jnp.broadcast_to(lowest, starts.shape)
    alive = alive[0:1, :]
    block = lax.broadcasted_iota(jnp.int32, (padded, total), 0)
    hits = jnp.where(block == mine, alive, 0.0)
    counts = jnp.sum(hits, axis=1, keepdims=True)
    before = jnp.sum(jnp.where(block == mine + 1, alive, 0.0), axis=1, keepdims=True)
    rows = counts * by_column[:, :half] + before * by_column[:, half:]
    inside = lax.broadcasted_iota(jnp.int32, (padded, half), 0) < blocks
    inverse[...] = jnp.where(inside, 1.0 / jnp.maximum(rows, row_floor), 0.0)
    ones = jnp.ones((8, table.shape[1]), table.dtype)
    by_voxel = lax.dot_general(
        ones, table, (((1,), (1,)), ((), ())), preferred_element_type=jnp.float32
    )[0:1]
    scaled = by_voxel * SUM_SCALE
    whole = jnp.floor(scaled)
    low = jnp.floor((scaled - whole) * LOW_SCALE + 0.5)
    packed = jnp.concatenate(
        [whole[:, :half], whole[:, half:], low[:, :half], low[:, half:]], axis=0
    )
    sums[...] = jnp.concatenate([packed, jnp.zeros((4, half), jnp.float32)], axis=0)


def tap_terms(terms):
    rest = smoothing_taps()[RIM:]
    parts = []
    for _ in range(terms):
        part = rest.astype(jnp.bfloat16).astype(np.float64)
        parts.append([float(v) for v in part])
        rest = rest - part
    return parts


def build_taps(taps, half, terms):
    row = lax.broadcasted_iota(jnp.int32, (half, half), 0)
    column = lax.broadcasted_iota(jnp.int32, (half, half), 1)
    parts = tap_terms(terms)
    for shift in (-1, 0, 1):
        apart = jnp.abs(row - column + shift * half)
        for term in range(terms):
            value = jnp.zeros((half, half), jnp.float32)
            for distance in range(RIM + 1):
                value = jnp.where(apart == distance, parts[term][distance], value)
            value = value.astype(taps.dtype)
            for side in range(2):
                base = (4 * term + 1 + side + shift) * half
                taps[base : base + half, side * half : (side + 1) * half] = value
    nothing = jnp.zeros((half, half), taps.dtype)
    for term in range(terms):
        taps[4 * term * half : (4 * term + 1) * half, half:] = nothing
        taps[(4 * term + 3) * half : (4 * term + 4) * half, :half] = nothing


def phase_kernel(slots, alive, offset_rows, intensity, near_rows, far_rows, footprint, *refs):
    phase, inverse, sums, starts, padded, across, taps = refs
    rows, columns = intensity.shape
    half = footprint.shape[1] // 2
    blocks = columns // half
    even = lax.rem(lax.axis_index("row"), 2) == 0
    decay = float(np.exp(-1.0 / decay_length))
    centre = float(smoothing_taps()[RIM])
    tall = rows + 2 * HALO
    edge = jnp.zeros((tall, half), padded.dtype)
    padded[:, :half] = edge
    padded[:, half + columns :] = edge
    inner = slice(half, half + columns)
    padded[HALO : HALO + rows, inner] = intensity[...]
    near = near_rows[...].astype(jnp.float32)
    far = far_rows[...].astype(jnp.float32)
    padded[:HALO, inner] = jnp.where(even, far, near).astype(padded.dtype)
    padded[HALO + rows :, inner] = jnp.where(even, near, far).astype(padded.dtype)
    build_taps(taps, half, TERMS)
    tables(slots, blocks, offset_rows, alive, footprint[...], inverse, sums, starts)
    terms = TERMS
    pairs = blocks // 2
    group = max(d for d in range(1, min(GROUP, pairs) + 1) if pairs % d == 0)
    stride = rows // 8

    def step(g, carry):
        tiles = [
            padded[:, pl.ds(pl.multiple_of((g * group + i) * 2 * half, half), 4 * half)]
            for i in range(group)
        ]
        stacked = jnp.concatenate([jnp.concatenate(tiles, axis=0)] * terms, axis=1)
        filtered = jnp.dot(stacked, taps[...], preferred_element_type=jnp.float32)
        for i in range(group):
            for h in range(2):
                across[(g * group + i) * 2 + h] = filtered[
                    i * tall : (i + 1) * tall, h * half : (h + 1) * half
                ]
        for i in range(2 * group):
            block = g * 2 * group + i
            lines = [
                across[block, pl.ds(HALO - RIM + m, 8, stride=stride), :]
                for m in range(stride + 2 * RIM)
            ]
            for k in range(stride):
                mid = k + RIM
                total = lines[mid - RIM] + lines[mid + RIM]
                for m in range(RIM - 1, 0, -1):
                    total = total * decay + (lines[mid - m] + lines[mid + m])
                total = total * decay + lines[mid]
                phase[block, pl.ds(k, 8, stride=stride), :] = -jnp.log(total * centre)
        return carry

    lax.fori_loop(0, pairs // group, step, 0)


def write_kernel(count, slots, offsets, tile_count, residual, out, plan):
    member = lax.axis_index("tile")
    lane = lax.broadcasted_iota(jnp.int32, (1, plan.shape[1]), 1)

    def one(angle, carry):
        start = group_start(offsets, angle, member, slots)
        row = jnp.zeros((1, plan.shape[1]), jnp.int32)
        for j in range(slots):
            row = jnp.where(lane == j, offsets[angle, member * slots + j] - start, row)
        plan[pl.ds(angle, 1), :] = row
        return carry

    lax.fori_loop(0, count, one, 0)
    plan[count : count + 1, :] = (lane < tile_count[member]).astype(jnp.int32)
    blocks, _, half = residual.shape
    for block in range(blocks):
        out[:, block * half : (block + 1) * half] = residual[block]


def encode(window, table, sums, piece):
    rows = window.shape[0]
    half = table.shape[1] // 2
    stacked = jnp.concatenate(
        [window[:, s * half : (s + 2) * half] for s in range(SPREAD)], axis=0
    )
    back = lax.dot_general(
        stacked, table, (((1,), (1,)), ((), ())), preferred_element_type=jnp.float32
    )
    top = jnp.max(jnp.max(jnp.abs(back), axis=0, keepdims=True), axis=1, keepdims=True)
    power = jnp.floor(jnp.log2(CODE_TOP / jnp.maximum(top, 1e-30)))
    code = jnp.round(back * jnp.exp2(power)).astype(jnp.int32)
    for s in range(SPREAD):
        for h in range(2):
            base = (2 * s + h) * rows
            piece[base : base + rows, :] = code[
                s * rows : (s + 1) * rows, h * half : (h + 1) * half
            ].astype(piece.dtype)
    base = 2 * SPREAD * rows
    line = lax.broadcasted_iota(jnp.int32, (EXTRA_ROWS, half), 0)
    extra = jnp.where(line < 4, sums, jnp.broadcast_to(power, (EXTRA_ROWS, half)))
    piece[base : base + EXTRA_ROWS, :] = extra.astype(jnp.int32).astype(piece.dtype)


def subtract_loads(ks, starts, arrived, table, residual, images):
    member = lax.axis_index("tile")
    blocks, rows, half = residual.shape

    def project(piece, image):
        image[...] = jnp.dot(
            piece[...].reshape(SPREAD * rows, table.shape[0]),
            table,
            preferred_element_type=jnp.float32,
        )

    def subtract(image, group):
        start = starts[group, 0]
        for s in range(SPREAD + 1):
            part = None
            if s < SPREAD:
                part = image[s * rows : (s + 1) * rows, :half]
            if s > 0:
                far = image[(s - 1) * rows : s * rows, half:]
                part = far if part is None else part + far
            block = start + s
            if s == SPREAD:
                part = jnp.where(block < blocks, part, 0.0)
                block = jnp.minimum(block, blocks - 1)
            residual[block] = residual[block] - part

    if len(arrived) == len(ks):
        for i, piece in enumerate(arrived):
            project(piece, images.at[i])
        for i, k in enumerate(ks):
            subtract(images.at[i], member ^ k)
    else:

        def one(k, carry):
            project(arrived[0].at[k], images.at[0])
            subtract(images.at[0], k)
            return carry

        lax.fori_loop(0, len(ks), one, 0)


def early_kernel(ks, starts, phase, footprint, *refs):
    arrived, residual, images = refs[: len(ks)], refs[-2], refs[-1]
    subtract_loads(ks, starts, arrived, footprint[...], residual, images)


def angle_kernel(direct, count, ks, first, starts, phase, footprint, inverse, sums, *refs):
    lists = len(ks) if direct else 1
    arrived, residual, windows = refs[:lists], refs[lists], refs[lists + 1]
    sent, images = refs[lists + 2 : -1], refs[-1]
    member = lax.axis_index("tile")
    table = footprint[...]
    blocks, _, half = phase.shape
    subtract_loads(ks, starts, arrived, table, residual, images)

    def weigh(window, group):
        start = starts[group, 0]
        for s in range(SPREAD + 1):
            block = jnp.minimum(start + s, blocks - 1)
            scale = inverse[pl.ds(start + s, 1), :]
            window[:, s * half : (s + 1) * half] = (residual[block] * scale).astype(window.dtype)

    if direct:
        for k in first:
            weigh(windows.at[k], member ^ k)
        for piece, k in zip(sent, first):
            encode(windows[k], table, sums[...], piece)
        for k in range(count):
            if k not in first:
                weigh(windows.at[k], member ^ k)
    else:

        def step(k, carry):
            weigh(windows.at[k], k)
            encode(windows[k], table, sums[...], sent[0].at[k])
            return carry

        lax.fori_loop(0, count, step, 0)


def back_kernel(ks, windows, footprint, sums, *sent):
    for piece, k in zip(sent, ks):
        encode(windows[k], footprint[...], sums[...], piece)


def gather_kernel(direct, count, ks, slots, rows, last, plan, *refs):
    lists = len(ks) if direct else 1
    received = refs[:lists]
    refs = refs[lists:]
    earlier = None
    if direct and last:
        earlier, earlier_sums, refs = refs[0], refs[1], refs[2:]
    correction, column_sums, decoded = refs
    member = lax.axis_index("tile")
    half = column_sums.shape[1]
    base = 2 * SPREAD * rows

    def unpack(piece, into):
        extra = piece[base : base + EXTRA_ROWS, :].astype(jnp.float32)
        into[...] = piece[0:base, :].astype(jnp.float32) * jnp.exp2(-extra[4:5])
        return (extra[0:2] + extra[2:4] * (1.0 / LOW_SCALE)) * (1.0 / SUM_SCALE)

    def block_of(into, angle, j):
        at = plan[angle, j] * (2 * rows)
        return into[pl.ds(pl.multiple_of(at, 2 * rows), 2 * rows), :]

    if direct:
        total = earlier_sums[0:2] if last else jnp.zeros((2, half), jnp.float32)
        angles = [member ^ k for k in ks]
        for i, piece in enumerate(received):
            total = total + unpack(piece, decoded.at[i])
    else:
        column_sums[...] = jnp.zeros_like(column_sums)
        correction[...] = jnp.zeros_like(correction)

        def step(k, carry):
            column_sums[0:2] += unpack(received[0].at[k], decoded.at[0])
            for j in range(slots):
                correction[j] += block_of(decoded.at[0], k, j)
            return carry

        lax.fori_loop(0, len(ks), step, 0)
        total = column_sums[0:2]

    if last:
        inverse = 1.0 / total
    else:
        column_sums[0:2] = total
    for j in range(slots):
        if direct:
            sum_here = earlier[j] if last else None
            for i, angle in enumerate(angles):
                part = block_of(decoded.at[i], angle, j)
                sum_here = part if sum_here is None else sum_here + part
        else:
            sum_here = correction[j]
        if not last:
            correction[j] = sum_here
        elif direct:
            weight = jnp.where(plan[count, j] > 0, 1.0, 0.0)
            for h in range(2):
                correction[j, :, h * half : (h + 1) * half] = sum_here[
                    h * rows : (h + 1) * rows
                ] * (inverse[h : h + 1] * weight)
        else:
            weight = jnp.where(plan[count, j] > 0, 1.0, 0.0)
            correction[j] = sum_here * weight * jnp.concatenate(
                [jnp.broadcast_to(inverse[h : h + 1], (rows, half)) for h in range(2)], axis=0
            )


def exchange(direct, count, pieces):
    if not direct:
        return [lax.all_to_all(pieces[0], "tile", split_axis=0, concat_axis=0, tiled=True)]
    arrived = [pieces[0]]
    for k in range(1, count):
        arrived.append(lax.ppermute(pieces[k], "tile", [(i, i ^ k) for i in range(count)]))
    return arrived


def partner_order(count, wanted):
    known = [k for k in wanted if 0 < k < count]
    return known + [k for k in range(count - 1, 0, -1) if k not in known]


def swap_halos(near_rows, far_rows):
    count = lax.axis_size("row")
    pairs = [(i, i + 1) for i in range(0, count - 1, 2)]
    between = [(i, i + 1) for i in range(1, count - 1, 2)]
    far_rows = lax.ppermute(far_rows, "row", between + [(b, a) for a, b in between])
    near_rows = lax.ppermute(near_rows, "row", pairs + [(b, a) for a, b in pairs])
    return near_rows, far_rows


def use_direct(count):
    return count <= DIRECT_LIMIT and count & (count - 1) == 0


def local(intensity, volume, footprint, foot_offset, tile_count):
    count = lax.axis_size("tile")
    direct = use_direct(count)
    slots, rows, voxels = volume.shape
    angles_here, _, window = footprint.shape
    assert angles_here == 1
    half = window // 2
    columns = intensity.shape[2]
    blocks = columns // half
    padded_blocks = -(-(blocks + SPREAD + 1) // 8) * 8
    offsets = jnp.transpose(foot_offset)
    table = footprint[0]

    def piece_shapes(shape, dtype):
        if direct:
            return [jax.ShapeDtypeStruct(shape, dtype)] * count
        return [jax.ShapeDtypeStruct((count,) + shape, dtype)]

    halo_shape = jax.ShapeDtypeStruct((HALO, columns), intensity.dtype)
    load_shapes = piece_shapes((SPREAD, rows, voxels), jnp.bfloat16)
    near_rows, far_rows, table, offset_rows, alive, *loads = pl.pallas_call(
        lambda *refs: load_kernel(direct, count, slots, *refs),
        out_shape=[halo_shape, halo_shape]
        + [jax.ShapeDtypeStruct(x.shape, x.dtype) for x in (table, offsets)]
        + [jax.ShapeDtypeStruct((8, offsets.shape[1]), jnp.float32)]
        + load_shapes,
        in_specs=[HBM] * 5,
        out_specs=[VMEM] * (5 + len(load_shapes)),
        scratch_shapes=[
            pltpu.SMEM(offsets.shape, jnp.int32),
            pltpu.SMEM(tile_count.shape, jnp.int32),
            pltpu.VMEM(volume.shape, volume.dtype),
            pltpu.SemaphoreType.DMA((7 + slots,)),
        ],
        compiler_params=params(16),
        name="loads",
    )(*[pltpu.with_memory_space_constraint(x, pltpu.HBM) for x in (offsets, tile_count, volume, table, intensity[0])])
    near_rows, far_rows = swap_halos(near_rows, far_rows)
    arrived = exchange(direct, count, loads)

    tall = rows + 2 * HALO
    phase_map, inverse, sums, starts = pl.pallas_call(
        lambda *refs: phase_kernel(slots, *refs),
        out_shape=[
            jax.ShapeDtypeStruct((blocks, rows, half), jnp.float32),
            jax.ShapeDtypeStruct((padded_blocks, half), jnp.float32),
            jax.ShapeDtypeStruct((EXTRA_ROWS, half), jnp.float32),
            jax.ShapeDtypeStruct((-(-count // 8) * 8, half), jnp.int32),
        ],
        in_specs=[VMEM] * 6,
        out_specs=[VMEM] * 4,
        scratch_shapes=[
            pltpu.VMEM((tall, columns + 2 * half), intensity.dtype),
            pltpu.VMEM((blocks, tall, half), jnp.float32),
            pltpu.VMEM((4 * TERMS * half, 2 * half), jnp.bfloat16),
        ],
        compiler_params=params(16),
        name="phase",
    )(alive, offset_rows, intensity[0], near_rows, far_rows, table)

    piece_shape = (2 * SPREAD * rows + EXTRA_ROWS, half)
    one_piece = jax.ShapeDtypeStruct(piece_shape, jnp.int16)
    first = partner_order(count, HOME_ORDER)[:FIRST] if direct else []
    rest = [k for k in range(count) if k not in first]
    sent_shapes = [one_piece] * len(first) if direct else piece_shapes(piece_shape, jnp.int16)
    grid_shape = jax.ShapeDtypeStruct((blocks, rows, half), jnp.float32)
    late = partner_order(count, OUT_ORDER)[-LATE:] if direct else list(range(count))
    if direct:
        early = [k for k in range(count) if k not in late]
        phase_map = pl.pallas_call(
            lambda *refs: early_kernel(early, *refs),
            out_shape=grid_shape,
            in_specs=[VMEM] * (3 + len(early)),
            out_specs=VMEM,
            scratch_shapes=[pltpu.VMEM((len(early), SPREAD * rows, voxels), jnp.float32)],
            input_output_aliases={1: 0},
            compiler_params=params(16),
            name="early",
        )(starts, phase_map, table, *[arrived[k] for k in early])
        arrived = [arrived[k] for k in late]
    residual, windows, *sent = pl.pallas_call(
        lambda *refs: angle_kernel(direct, count, late, first, *refs),
        out_shape=[
            grid_shape,
            jax.ShapeDtypeStruct((count, rows, (SPREAD + 1) * half), jnp.bfloat16),
        ]
        + sent_shapes,
        in_specs=[VMEM] * (5 + len(arrived)),
        out_specs=[VMEM] * (2 + len(sent_shapes)),
        scratch_shapes=[
            pltpu.VMEM((len(arrived), SPREAD * rows, voxels), jnp.float32),
        ],
        input_output_aliases={1: 0},
        compiler_params=params(16),
        name="angle",
    )(starts, phase_map, table, inverse, sums, *arrived)
    if direct:
        others = pl.pallas_call(
            lambda *refs: back_kernel(rest, *refs),
            out_shape=[one_piece] * len(rest),
            in_specs=[VMEM] * 3,
            out_specs=[VMEM] * len(rest),
            compiler_params=params(16),
            name="back",
        )(windows, table, sums)
        by_partner = dict(zip(first + rest, [*sent, *others]))
        sent = [by_partner[k] for k in range(count)]
    received = exchange(direct, count, sent)

    residual, plan = pl.pallas_call(
        lambda *refs: write_kernel(count, slots, *refs),
        out_shape=[
            jax.ShapeDtypeStruct((rows, columns), jnp.float32),
            jax.ShapeDtypeStruct((count + 8, half), jnp.int32),
        ],
        in_specs=[SMEM, SMEM, VMEM],
        out_specs=[VMEM, VMEM],
        compiler_params=params(16),
        name="write",
    )(offset_rows, tile_count, residual)

    def gather(ks, pieces, last, *earlier):
        flat = (slots, 2 * rows, half)
        shape = (slots, rows, voxels) if direct and last else flat
        return pl.pallas_call(
            lambda *refs: gather_kernel(direct, count, ks, slots, rows, last, *refs),
            out_shape=[
                jax.ShapeDtypeStruct(shape, jnp.float32),
                jax.ShapeDtypeStruct((8, half), jnp.float32),
            ],
            in_specs=[VMEM] * (1 + len(pieces) + len(earlier)),
            out_specs=[VMEM, VMEM],
            scratch_shapes=[
                pltpu.VMEM((len(pieces), 2 * SPREAD * rows, half), jnp.float32),
            ],
            compiler_params=params(16),
            name="gather_last" if last else "gather_first",
        )(plan, *pieces, *earlier)

    if direct:
        last = [0] + partner_order(count, HOME_ORDER)[-LATE:]
        soon = [k for k in range(count) if k not in last]
        partial = gather(soon, [received[k] for k in soon], False)
        correction = gather(last, [received[k] for k in last], True, *partial)[0]
    else:
        flat = gather(list(range(count)), received, True)[0]
        correction = jnp.swapaxes(flat.reshape(slots, 2, rows, half), 1, 2)
        correction = correction.reshape(slots, rows, voxels)
    return residual[None], correction


def solution(mesh):
    placed = (P("tile", "row", None), P("tile", "row", None), P("tile", None, None), P(), P())
    return jax.shard_map(
        local,
        mesh=mesh,
        in_specs=placed,
        out_specs=(P("tile", "row", None), P("tile", "row", None)),
        check_vma=False,
    )
```

```python
import jax
import jax.numpy as jnp
import numpy as np
from jax import lax
from jax.experimental import pallas as pl
from jax.experimental.pallas import tpu as pltpu
from jax.sharding import PartitionSpec as P


SPREAD = 4
RIM = 3
HALO = 8
GROUP = 22
TERMS = 2
FIRST = 2
LATE = 3
OUT_ORDER = (7, 5, 6, 4, 3, 2, 1)
HOME_ORDER = (6, 5, 7, 4, 3, 2, 1)
DIRECT_LIMIT = 16
EXTRA_ROWS = 8
SUM_SCALE = 2048.0
LOW_SCALE = 32000.0
CODE_TOP = 32000.0

decay_length = 2.0
row_floor = 0.5


SMEM = pl.BlockSpec(memory_space=pltpu.SMEM)
VMEM = pl.BlockSpec(memory_space=pltpu.VMEM)
HBM = pl.BlockSpec(memory_space=pltpu.HBM)


def params(mib):
    return pltpu.CompilerParams(vmem_limit_bytes=mib << 20)


def smoothing_taps():
    spread_taps = np.exp(-np.abs(np.arange(-RIM, RIM + 1)) / decay_length)
    return spread_taps / spread_taps.sum()


def each_piece(direct, count, member, refs, body):
    if direct:
        for k in range(count):
            body(refs[k], member ^ k)
    else:

        def step(k, carry):
            body(refs[0].at[k], k)
            return carry

        lax.fori_loop(0, count, step, 0)


def group_start(offsets, angle, group, slots):
    low = offsets[angle, group * slots]
    for j in range(1, slots):
        low = jnp.minimum(low, offsets[angle, group * slots + j])
    return low


def load_kernel(
    direct, count, slots, offsets_in, count_in, volume_in, table_in, intensity, *refs
):
    lists = count if direct else 1
    near_rows, far_rows, table_out, offsets_out, alive = refs[:5]
    pieces = refs[5 : 5 + lists]
    offsets, tile_count, volume, sems = refs[5 + lists :]
    member = lax.axis_index("tile")
    even = lax.rem(lax.axis_index("row"), 2) == 0
    last = intensity.shape[0] - HALO
    first_copy = pltpu.make_async_copy(offsets_in, offsets, sems.at[0])
    count_copy = pltpu.make_async_copy(count_in, tile_count, sems.at[1])
    near = pl.multiple_of(jnp.where(even, last, 0), HALO)
    far = pl.multiple_of(jnp.where(even, 0, last), HALO)
    near_copy = pltpu.make_async_copy(intensity.at[pl.ds(near, HALO)], near_rows, sems.at[3])
    far_copy = pltpu.make_async_copy(intensity.at[pl.ds(far, HALO)], far_rows, sems.at[4])
    table_copy = pltpu.make_async_copy(table_in, table_out, sems.at[5])
    rows_copy = pltpu.make_async_copy(offsets_in, offsets_out, sems.at[6])
    later = [near_copy, far_copy, table_copy, rows_copy]
    volume_copies = [
        pltpu.make_async_copy(volume_in.at[j], volume.at[j], sems.at[7 + j]) for j in range(slots)
    ]
    for copy in volume_copies:
        copy.start()
    first_copy.start()
    count_copy.start()
    for copy in later:
        copy.start()
    first_copy.wait()
    count_copy.wait()
    live = tile_count[member]
    for copy in volume_copies:
        copy.wait()

    whole = jnp.zeros(volume.shape[1:], jnp.float32)
    for j in range(slots):
        whole = whole + jnp.where(j < live, 1.0, 0.0) * volume[j]

    def one(piece, angle):
        start = group_start(offsets, angle, member, slots)
        places = [offsets[angle, member * slots + j] - start for j in range(slots)]
        places = [jnp.where(j < live, places[j], -1) for j in range(slots)]
        rest = whole
        for s in range(SPREAD - 1):
            total = jnp.zeros(volume.shape[1:], jnp.float32)
            for j in range(slots):
                total = total + jnp.where(places[j] == s, 1.0, 0.0) * volume[j]
            piece[s] = total.astype(piece.dtype)
            rest = rest - total
        piece[SPREAD - 1] = rest.astype(piece.dtype)

    each_piece(direct, count, member, pieces, one)
    lane = lax.broadcasted_iota(jnp.int32, alive.shape, 1)
    flags = jnp.zeros(alive.shape, jnp.float32)
    for g in range(alive.shape[1] // slots):
        here = (lane >= g * slots) & (lane < g * slots + tile_count[g])
        flags = jnp.where(here, 1.0, flags)
    alive[...] = flags
    for copy in later:
        copy.wait()


def tables(slots, blocks, offset_rows, alive, table, inverse, sums, starts):
    member = lax.axis_index("tile")
    half = table.shape[1] // 2
    padded = inverse.shape[0]
    total = offset_rows.shape[1]
    by_column = jnp.sum(table.astype(jnp.float32), axis=0, keepdims=True)
    mine = offset_rows[pl.ds(member, 1), :]
    group = lax.broadcasted_iota(jnp.int32, (starts.shape[0], total), 0)
    lane = lax.broadcasted_iota(jnp.int32, (starts.shape[0], total), 1)
    own = (lane >= group * slots) & (lane < (group + 1) * slots)
    lowest = jnp.min(jnp.where(own, mine, 1 << 20), axis=1, keepdims=True)
    starts[...] = jnp.broadcast_to(lowest, starts.shape)
    alive = alive[0:1, :]
    block = lax.broadcasted_iota(jnp.int32, (padded, total), 0)
    hits = jnp.where(block == mine, alive, 0.0)
    counts = jnp.sum(hits, axis=1, keepdims=True)
    before = jnp.sum(jnp.where(block == mine + 1, alive, 0.0), axis=1, keepdims=True)
    rows = counts * by_column[:, :half] + before * by_column[:, half:]
    inside = lax.broadcasted_iota(jnp.int32, (padded, half), 0) < blocks
    inverse[...] = jnp.where(inside, 1.0 / jnp.maximum(rows, row_floor), 0.0)
    ones = jnp.ones((8, table.shape[1]), table.dtype)
    by_voxel = lax.dot_general(
        ones, table, (((1,), (1,)), ((), ())), preferred_element_type=jnp.float32
    )[0:1]
    scaled = by_voxel * SUM_SCALE
    whole = jnp.floor(scaled)
    low = jnp.floor((scaled - whole) * LOW_SCALE + 0.5)
    packed = jnp.concatenate(
        [whole[:, :half], whole[:, half:], low[:, :half], low[:, half:]], axis=0
    )
    sums[...] = jnp.concatenate([packed, jnp.zeros((4, half), jnp.float32)], axis=0)


def tap_terms(terms):
    rest = smoothing_taps()[RIM:]
    parts = []
    for _ in range(terms):
        part = rest.astype(jnp.bfloat16).astype(np.float64)
        parts.append([float(v) for v in part])
        rest = rest - part
    return parts


def build_taps(taps, half, terms):
    row = lax.broadcasted_iota(jnp.int32, (half, half), 0)
    column = lax.broadcasted_iota(jnp.int32, (half, half), 1)
    parts = tap_terms(terms)
    for shift in (-1, 0, 1):
        apart = jnp.abs(row - column + shift * half)
        for term in range(terms):
            value = jnp.zeros((half, half), jnp.float32)
            for distance in range(RIM + 1):
                value = jnp.where(apart == distance, parts[term][distance], value)
            value = value.astype(taps.dtype)
            for side in range(2):
                base = (4 * term + 1 + side + shift) * half
                taps[base : base + half, side * half : (side + 1) * half] = value
    nothing = jnp.zeros((half, half), taps.dtype)
    for term in range(terms):
        taps[4 * term * half : (4 * term + 1) * half, half:] = nothing
        taps[(4 * term + 3) * half : (4 * term + 4) * half, :half] = nothing


def phase_kernel(slots, alive, offset_rows, intensity, near_rows, far_rows, footprint, *refs):
    phase, inverse, sums, starts, padded, across, taps = refs
    rows, columns = intensity.shape
    half = footprint.shape[1] // 2
    blocks = columns // half
    even = lax.rem(lax.axis_index("row"), 2) == 0
    decay = float(np.exp(-1.0 / decay_length))
    centre = float(smoothing_taps()[RIM])
    tall = rows + 2 * HALO
    edge = jnp.zeros((tall, half), padded.dtype)
    padded[:, :half] = edge
    padded[:, half + columns :] = edge
    inner = slice(half, half + columns)
    padded[HALO : HALO + rows, inner] = intensity[...]
    near = near_rows[...].astype(jnp.float32)
    far = far_rows[...].astype(jnp.float32)
    padded[:HALO, inner] = jnp.where(even, far, near).astype(padded.dtype)
    padded[HALO + rows :, inner] = jnp.where(even, near, far).astype(padded.dtype)
    build_taps(taps, half, TERMS)
    tables(slots, blocks, offset_rows, alive, footprint[...], inverse, sums, starts)
    terms = TERMS
    pairs = blocks // 2
    group = max(d for d in range(1, min(GROUP, pairs) + 1) if pairs % d == 0)
    stride = rows // 8

    def step(g, carry):
        tiles = [
            padded[:, pl.ds(pl.multiple_of((g * group + i) * 2 * half, half), 4 * half)]
            for i in range(group)
        ]
        stacked = jnp.concatenate([jnp.concatenate(tiles, axis=0)] * terms, axis=1)
        filtered = jnp.dot(stacked, taps[...], preferred_element_type=jnp.float32)
        for i in range(group):
            for h in range(2):
                across[(g * group + i) * 2 + h] = filtered[
                    i * tall : (i + 1) * tall, h * half : (h + 1) * half
                ]
        for i in range(2 * group):
            block = g * 2 * group + i
            lines = [
                across[block, pl.ds(HALO - RIM + m, 8, stride=stride), :]
                for m in range(stride + 2 * RIM)
            ]
            for k in range(stride):
                mid = k + RIM
                total = lines[mid - RIM] + lines[mid + RIM]
                for m in range(RIM - 1, 0, -1):
                    total = total * decay + (lines[mid - m] + lines[mid + m])
                total = total * decay + lines[mid]
                phase[block, pl.ds(k, 8, stride=stride), :] = -jnp.log(total * centre)
        return carry

    lax.fori_loop(0, pairs // group, step, 0)


def write_kernel(count, slots, offsets, tile_count, residual, out, plan):
    member = lax.axis_index("tile")
    lane = lax.broadcasted_iota(jnp.int32, (1, plan.shape[1]), 1)

    def one(angle, carry):
        start = group_start(offsets, angle, member, slots)
        row = jnp.zeros((1, plan.shape[1]), jnp.int32)
        for j in range(slots):
            row = jnp.where(lane == j, offsets[angle, member * slots + j] - start, row)
        plan[pl.ds(angle, 1), :] = row
        return carry

    lax.fori_loop(0, count, one, 0)
    plan[count : count + 1, :] = (lane < tile_count[member]).astype(jnp.int32)
    blocks, _, half = residual.shape
    for block in range(blocks):
        out[:, block * half : (block + 1) * half] = residual[block]


def encode(window, table, sums, piece):
    rows = window.shape[0]
    half = table.shape[1] // 2
    stacked = jnp.concatenate(
        [window[:, s * half : (s + 2) * half] for s in range(SPREAD)], axis=0
    )
    back = lax.dot_general(
        stacked, table, (((1,), (1,)), ((), ())), preferred_element_type=jnp.float32
    )
    top = jnp.max(jnp.max(jnp.abs(back), axis=0, keepdims=True), axis=1, keepdims=True)
    power = jnp.floor(jnp.log2(CODE_TOP / jnp.maximum(top, 1e-30)))
    code = jnp.round(back * jnp.exp2(power)).astype(jnp.int32)
    for s in range(SPREAD):
        for h in range(2):
            base = (2 * s + h) * rows
            piece[base : base + rows, :] = code[
                s * rows : (s + 1) * rows, h * half : (h + 1) * half
            ].astype(piece.dtype)
    base = 2 * SPREAD * rows
    line = lax.broadcasted_iota(jnp.int32, (EXTRA_ROWS, half), 0)
    extra = jnp.where(line < 4, sums, jnp.broadcast_to(power, (EXTRA_ROWS, half)))
    piece[base : base + EXTRA_ROWS, :] = extra.astype(jnp.int32).astype(piece.dtype)


def subtract_loads(ks, starts, arrived, table, residual, images):
    member = lax.axis_index("tile")
    blocks, rows, half = residual.shape

    def project(piece, image):
        image[...] = jnp.dot(
            piece[...].reshape(SPREAD * rows, table.shape[0]),
            table,
            preferred_element_type=jnp.float32,
        )

    def subtract(image, group):
        start = starts[group, 0]
        for s in range(SPREAD + 1):
            part = None
            if s < SPREAD:
                part = image[s * rows : (s + 1) * rows, :half]
            if s > 0:
                far = image[(s - 1) * rows : s * rows, half:]
                part = far if part is None else part + far
            block = start + s
            if s == SPREAD:
                part = jnp.where(block < blocks, part, 0.0)
                block = jnp.minimum(block, blocks - 1)
            residual[block] = residual[block] - part

    if len(arrived) == len(ks):
        for i, piece in enumerate(arrived):
            project(piece, images.at[i])
        for i, k in enumerate(ks):
            subtract(images.at[i], member ^ k)
    else:

        def one(k, carry):
            project(arrived[0].at[k], images.at[0])
            subtract(images.at[0], k)
            return carry

        lax.fori_loop(0, len(ks), one, 0)


def early_kernel(ks, starts, phase, footprint, *refs):
    arrived, residual, images = refs[: len(ks)], refs[-2], refs[-1]
    subtract_loads(ks, starts, arrived, footprint[...], residual, images)


def angle_kernel(direct, count, ks, first, starts, phase, footprint, inverse, sums, *refs):
    lists = len(ks) if direct else 1
    arrived, residual, windows = refs[:lists], refs[lists], refs[lists + 1]
    sent, images = refs[lists + 2 : -1], refs[-1]
    member = lax.axis_index("tile")
    table = footprint[...]
    blocks, _, half = phase.shape
    subtract_loads(ks, starts, arrived, table, residual, images)

    def weigh(window, group):
        start = starts[group, 0]
        for s in range(SPREAD + 1):
            block = jnp.minimum(start + s, blocks - 1)
            scale = inverse[pl.ds(start + s, 1), :]
            window[:, s * half : (s + 1) * half] = (residual[block] * scale).astype(window.dtype)

    if direct:
        for k in first:
            weigh(windows.at[k], member ^ k)
        for piece, k in zip(sent, first):
            encode(windows[k], table, sums[...], piece)
        for k in range(count):
            if k not in first:
                weigh(windows.at[k], member ^ k)
    else:

        def step(k, carry):
            weigh(windows.at[k], k)
            encode(windows[k], table, sums[...], sent[0].at[k])
            return carry

        lax.fori_loop(0, count, step, 0)


def back_kernel(ks, windows, footprint, sums, *sent):
    for piece, k in zip(sent, ks):
        encode(windows[k], footprint[...], sums[...], piece)


def gather_kernel(direct, count, ks, slots, rows, last, plan, *refs):
    lists = len(ks) if direct else 1
    received = refs[:lists]
    refs = refs[lists:]
    earlier = None
    if direct and last:
        earlier, earlier_sums, refs = refs[0], refs[1], refs[2:]
    correction, column_sums, decoded = refs
    member = lax.axis_index("tile")
    half = column_sums.shape[1]
    base = 2 * SPREAD * rows

    def unpack(piece, into):
        extra = piece[base : base + EXTRA_ROWS, :].astype(jnp.float32)
        into[...] = piece[0:base, :].astype(jnp.float32) * jnp.exp2(-extra[4:5])
        return (extra[0:2] + extra[2:4] * (1.0 / LOW_SCALE)) * (1.0 / SUM_SCALE)

    def block_of(into, angle, j):
        at = plan[angle, j] * (2 * rows)
        return into[pl.ds(pl.multiple_of(at, 2 * rows), 2 * rows), :]

    if direct:
        total = earlier_sums[0:2] if last else jnp.zeros((2, half), jnp.float32)
        angles = [member ^ k for k in ks]
        for i, piece in enumerate(received):
            total = total + unpack(piece, decoded.at[i])
    else:
        column_sums[...] = jnp.zeros_like(column_sums)
        correction[...] = jnp.zeros_like(correction)

        def step(k, carry):
            column_sums[0:2] += unpack(received[0].at[k], decoded.at[0])
            for j in range(slots):
                correction[j] += block_of(decoded.at[0], k, j)
            return carry

        lax.fori_loop(0, len(ks), step, 0)
        total = column_sums[0:2]

    if last:
        inverse = 1.0 / total
    else:
        column_sums[0:2] = total
    for j in range(slots):
        if direct:
            sum_here = earlier[j] if last else None
            for i, angle in enumerate(angles):
                part = block_of(decoded.at[i], angle, j)
                sum_here = part if sum_here is None else sum_here + part
        else:
            sum_here = correction[j]
        if not last:
            correction[j] = sum_here
        elif direct:
            weight = jnp.where(plan[count, j] > 0, 1.0, 0.0)
            for h in range(2):
                correction[j, :, h * half : (h + 1) * half] = sum_here[
                    h * rows : (h + 1) * rows
                ] * (inverse[h : h + 1] * weight)
        else:
            weight = jnp.where(plan[count, j] > 0, 1.0, 0.0)
            correction[j] = sum_here * weight * jnp.concatenate(
                [jnp.broadcast_to(inverse[h : h + 1], (rows, half)) for h in range(2)], axis=0
            )


def exchange(direct, count, pieces):
    if not direct:
        return [lax.all_to_all(pieces[0], "tile", split_axis=0, concat_axis=0, tiled=True)]
    arrived = [pieces[0]]
    for k in range(1, count):
        arrived.append(lax.ppermute(pieces[k], "tile", [(i, i ^ k) for i in range(count)]))
    return arrived


def partner_order(count, wanted):
    known = [k for k in wanted if 0 < k < count]
    return known + [k for k in range(count - 1, 0, -1) if k not in known]


def swap_halos(near_rows, far_rows):
    count = lax.axis_size("row")
    pairs = [(i, i + 1) for i in range(0, count - 1, 2)]
    between = [(i, i + 1) for i in range(1, count - 1, 2)]
    far_rows = lax.ppermute(far_rows, "row", between + [(b, a) for a, b in between])
    near_rows = lax.ppermute(near_rows, "row", pairs + [(b, a) for a, b in pairs])
    return near_rows, far_rows


def use_direct(count):
    return count <= DIRECT_LIMIT and count & (count - 1) == 0


def local(intensity, volume, footprint, foot_offset, tile_count):
    count = lax.axis_size("tile")
    direct = use_direct(count)
    slots, rows, voxels = volume.shape
    angles_here, _, window = footprint.shape
    assert angles_here == 1
    half = window // 2
    columns = intensity.shape[2]
    blocks = columns // half
    padded_blocks = -(-(blocks + SPREAD + 1) // 8) * 8
    offsets = jnp.transpose(foot_offset)
    table = footprint[0]

    def piece_shapes(shape, dtype):
        if direct:
            return [jax.ShapeDtypeStruct(shape, dtype)] * count
        return [jax.ShapeDtypeStruct((count,) + shape, dtype)]

    halo_shape = jax.ShapeDtypeStruct((HALO, columns), intensity.dtype)
    load_shapes = piece_shapes((SPREAD, rows, voxels), jnp.bfloat16)
    near_rows, far_rows, table, offset_rows, alive, *loads = pl.pallas_call(
        lambda *refs: load_kernel(direct, count, slots, *refs),
        out_shape=[halo_shape, halo_shape]
        + [jax.ShapeDtypeStruct(x.shape, x.dtype) for x in (table, offsets)]
        + [jax.ShapeDtypeStruct((8, offsets.shape[1]), jnp.float32)]
        + load_shapes,
        in_specs=[HBM] * 5,
        out_specs=[VMEM] * (5 + len(load_shapes)),
        scratch_shapes=[
            pltpu.SMEM(offsets.shape, jnp.int32),
            pltpu.SMEM(tile_count.shape, jnp.int32),
            pltpu.VMEM(volume.shape, volume.dtype),
            pltpu.SemaphoreType.DMA((7 + slots,)),
        ],
        compiler_params=params(16),
        name="loads",
    )(*[pltpu.with_memory_space_constraint(x, pltpu.HBM) for x in (offsets, tile_count, volume, table, intensity[0])])
    near_rows, far_rows = swap_halos(near_rows, far_rows)
    arrived = exchange(direct, count, loads)
    intensity, near_rows = lax.optimization_barrier((intensity, near_rows))

    tall = rows + 2 * HALO
    phase_map, inverse, sums, starts = pl.pallas_call(
        lambda *refs: phase_kernel(slots, *refs),
        out_shape=[
            jax.ShapeDtypeStruct((blocks, rows, half), jnp.float32),
            jax.ShapeDtypeStruct((padded_blocks, half), jnp.float32),
            jax.ShapeDtypeStruct((EXTRA_ROWS, half), jnp.float32),
            jax.ShapeDtypeStruct((-(-count // 8) * 8, half), jnp.int32),
        ],
        in_specs=[VMEM] * 6,
        out_specs=[VMEM] * 4,
        scratch_shapes=[
            pltpu.VMEM((tall, columns + 2 * half), intensity.dtype),
            pltpu.VMEM((blocks, tall, half), jnp.float32),
            pltpu.VMEM((4 * TERMS * half, 2 * half), jnp.bfloat16),
        ],
        compiler_params=params(16),
        name="phase",
    )(alive, offset_rows, intensity[0], near_rows, far_rows, table)

    piece_shape = (2 * SPREAD * rows + EXTRA_ROWS, half)
    one_piece = jax.ShapeDtypeStruct(piece_shape, jnp.int16)
    first = partner_order(count, HOME_ORDER)[:FIRST] if direct else []
    rest = [k for k in range(count) if k not in first]
    sent_shapes = [one_piece] * len(first) if direct else piece_shapes(piece_shape, jnp.int16)
    grid_shape = jax.ShapeDtypeStruct((blocks, rows, half), jnp.float32)
    late = partner_order(count, OUT_ORDER)[-LATE:] if direct else list(range(count))
    if direct:
        early = [k for k in range(count) if k not in late]
        phase_map = pl.pallas_call(
            lambda *refs: early_kernel(early, *refs),
            out_shape=grid_shape,
            in_specs=[VMEM] * (3 + len(early)),
            out_specs=VMEM,
            scratch_shapes=[pltpu.VMEM((len(early), SPREAD * rows, voxels), jnp.float32)],
            input_output_aliases={1: 0},
            compiler_params=params(16),
            name="early",
        )(starts, phase_map, table, *[arrived[k] for k in early])
        arrived = [arrived[k] for k in late]
    residual, windows, *sent = pl.pallas_call(
        lambda *refs: angle_kernel(direct, count, late, first, *refs),
        out_shape=[
            grid_shape,
            jax.ShapeDtypeStruct((count, rows, (SPREAD + 1) * half), jnp.bfloat16),
        ]
        + sent_shapes,
        in_specs=[VMEM] * (5 + len(arrived)),
        out_specs=[VMEM] * (2 + len(sent_shapes)),
        scratch_shapes=[
            pltpu.VMEM((len(arrived), SPREAD * rows, voxels), jnp.float32),
        ],
        input_output_aliases={1: 0},
        compiler_params=params(16),
        name="angle",
    )(starts, phase_map, table, inverse, sums, *arrived)
    if direct:
        others = pl.pallas_call(
            lambda *refs: back_kernel(rest, *refs),
            out_shape=[one_piece] * len(rest),
            in_specs=[VMEM] * 3,
            out_specs=[VMEM] * len(rest),
            compiler_params=params(16),
            name="back",
        )(windows, table, sums)
        by_partner = dict(zip(first + rest, [*sent, *others]))
        sent = [by_partner[k] for k in range(count)]
    received = exchange(direct, count, sent)

    residual, plan = pl.pallas_call(
        lambda *refs: write_kernel(count, slots, *refs),
        out_shape=[
            jax.ShapeDtypeStruct((rows, columns), jnp.float32),
            jax.ShapeDtypeStruct((count + 8, half), jnp.int32),
        ],
        in_specs=[SMEM, SMEM, VMEM],
        out_specs=[VMEM, VMEM],
        compiler_params=params(16),
        name="write",
    )(offset_rows, tile_count, residual)

    def gather(ks, pieces, last, *earlier):
        flat = (slots, 2 * rows, half)
        shape = (slots, rows, voxels) if direct and last else flat
        return pl.pallas_call(
            lambda *refs: gather_kernel(direct, count, ks, slots, rows, last, *refs),
            out_shape=[
                jax.ShapeDtypeStruct(shape, jnp.float32),
                jax.ShapeDtypeStruct((8, half), jnp.float32),
            ],
            in_specs=[VMEM] * (1 + len(pieces) + len(earlier)),
            out_specs=[VMEM, VMEM],
            scratch_shapes=[
                pltpu.VMEM((len(pieces), 2 * SPREAD * rows, half), jnp.float32),
            ],
            compiler_params=params(16),
            name="gather_last" if last else "gather_first",
        )(plan, *pieces, *earlier)

    if direct:
        last = [0] + partner_order(count, HOME_ORDER)[-LATE:]
        soon = [k for k in range(count) if k not in last]
        partial = gather(soon, [received[k] for k in soon], False)
        correction = gather(last, [received[k] for k in last], True, *partial)[0]
    else:
        flat = gather(list(range(count)), received, True)[0]
        correction = jnp.swapaxes(flat.reshape(slots, 2, rows, half), 1, 2)
        correction = correction.reshape(slots, rows, voxels)
    return residual[None], correction


def solution(mesh):
    placed = (P("tile", "row", None), P("tile", "row", None), P("tile", None, None), P(), P())
    return jax.shard_map(
        local,
        mesh=mesh,
        in_specs=placed,
        out_specs=(P("tile", "row", None), P("tile", "row", None)),
        check_vma=False,
    )
```
